128 devices in a mesh: group: 4 (over x), img: 32 (over z, y, core).
Axes of the slice: x: 4, y: 4, z: 4, core: 2. Of those that a mesh axis runs over, the one named last changes fastest.
Arguments:
- enc_tokens: bfloat16 [128, 768, 1024], P(('group', 'img')), may hold values from -6 to 6
- embed_weight: bfloat16 [1024, 768], replicated, may hold values from -0.1875 to 0.1875
- embed_bias: float32 [768], replicated, may hold values from -3 to 3
- query_gain: float32 [768], replicated, may hold values from 0.25 to 1.75
- memory_gain: float32 [768], replicated, may hold values from 0.25 to 1.75
- query_weight: bfloat16 [768, 768], replicated, may hold values from -0.43164062 to 0.43164062
- key_weight: bfloat16 [768, 768], replicated, may hold values from -0.21875 to 0.21875
- value_weight: bfloat16 [768, 768], replicated, may hold values from -0.21875 to 0.21875
- out_weight: bfloat16 [768, 768], replicated, may hold values from -0.43164062 to 0.43164062
- head_weight: bfloat16 [768, 512], replicated, may hold values from -0.21875 to 0.21875
- pair_dst: int32 [512], P(('group', 'img')), may hold values from 0 to 127, as said below
- pair_count: int32 [128], P(('group', 'img')), may hold values from 3 to 4, as said below
- depth: float32 [128, 768, 256], P(('group', 'img')), may hold values from -3 to 3
- scale: float32 [128], replicated, may hold values from -3 to 3
- focal: float32 [128], replicated, may hold values from -3 to 3
Outputs:
- pair_tokens: bfloat16 [512, 768, 768], P(('group', 'img'))
- depth_out: float32 [128, 768, 256], P(('group', 'img'))
- scale_out: float32 [128], replicated
- focal_out: float32 [128], replicated
The draws below stay inside these ranges and needn't reach their ends.
Inputs may be any that keep to these rules, and one draw needn't show every extreme that they name: `pair_dst`: each slot of the device at (group g, img j) names an image owned by the device at (g, j - 1), (g, j + 1), or (g - 1 wrapped over the group axis, j). The live slots of a device are its first pair_count slots.
All inputs are finite; a program needn't handle non-finite values.
Results may differ from the reference program's by a relative error of at most 0.008.
Values may be sent and summed in bfloat16 or wider, within the bound.
No kernel may reach another device: no remote copies, remote signals or barrier semaphores. Data moves between devices by JAX's collectives and lax.ppermute only.
A program may use at most 192 MiB of HBM per device.

```python
import jax
import jax.numpy as jnp
from jax import lax

DE = 1024
HEADS = 12
HD = 64
DD = 768
L = 768
PP = 256
IMG_DEV = 1
ITERS = 2
PAIR_CAP = 4
IMAGES = 128
PAIRS = 512
N_GROUP = 4
N_IMG = 32


def pair_plan(key):
    key = jax.random.fold_in(key, 11)
    devs = N_GROUP * N_IMG
    dev = jnp.arange(devs, dtype=jnp.int32)
    grp = dev // N_IMG
    col = dev % N_IMG
    right = jnp.where(col < N_IMG - 1, dev + 1, dev - 1)
    left = jnp.where(col > 0, dev - 1, dev + 1)
    cross = (grp + N_GROUP - 1) % N_GROUP * N_IMG + col
    key_pick, key_within, key_count, key_top, key_low = jax.random.split(key, 5)
    pick = jax.random.randint(key_pick, (devs, IMG_DEV), 0, 3)
    extra = jnp.where(pick == 0, left[:, None], jnp.where(pick == 1, right[:, None], cross[:, None]))
    owners = jnp.concatenate([jnp.broadcast_to(right[:, None], (devs, IMG_DEV)), jnp.broadcast_to(cross[:, None], (devs, IMG_DEV)), jnp.broadcast_to(left[:, None], (devs, IMG_DEV)), extra], axis=1)
    within = jax.random.randint(key_within, (devs, PAIR_CAP), 0, IMG_DEV)
    targets = (owners * IMG_DEV + within).astype(jnp.int32)
    counts = jax.random.randint(key_count, (devs,), 3 * IMG_DEV, PAIR_CAP + 1)
    top_dev = jax.random.randint(key_top, (), 0, devs)
    low_dev = (top_dev + 1 + jax.random.randint(key_low, (), 0, devs - 1)) % devs
    counts = counts.at[top_dev].set(PAIR_CAP).at[low_dev].set(3 * IMG_DEV)
    return (targets.reshape(-1), counts.astype(jnp.int32))


def draw_pair_dst(key, part):
    return pair_plan(key)[0]


def draw_pair_count(key, part):
    return pair_plan(key)[1]


def level_of(own_key, extent, shards, smallest, high):
    level, own = 1.0, jax.random.fold_in(own_key, 6)
    for position, parts in shards:
        heights = jnp.exp(jax.random.uniform(jax.random.fold_in(own, position), (parts,), jnp.float32, smallest / len(shards), high / len(shards)))
        level = level * jnp.repeat(heights, extent[position] // parts).reshape([-1 if axis == position else 1 for axis in range(len(extent))])
    return level


def scatter_about(stream_key, extent, width, bound, cuts=(), kind=jnp.bfloat16):
    values = jax.random.normal(stream_key, extent, jnp.float32) * width
    if len(cuts) > 0:
        values = level_of(stream_key, extent, cuts, -0.22, 0.18) * values
    return jnp.clip(values, min=-bound, max=bound).astype(kind)


def setup_inputs(seed: int = 0) -> dict:
    splits = jax.random.split(jax.random.key(seed), 16)
    enc_tokens = scatter_about(splits[0], (IMAGES, L, DE), 1.0, 6.0, ((0, 128),))
    embed_weight = scatter_about(splits[1], (DE, DD), DE ** -0.5, 0.1875)
    embed_bias = scatter_about(splits[2], (DD,), 0.5, 3.0, (), jnp.float32)
    query_gain = jnp.clip(1.0 + 0.15 * jax.random.normal(splits[3], (DD,), jnp.float32), 0.25, 1.75)
    memory_gain = jnp.clip(1.0 + 0.15 * jax.random.normal(splits[4], (DD,), jnp.float32), 0.25, 1.75)
    query_weight = scatter_about(splits[5], (DD, DD), (2.0 * DD ** -0.5), 0.43164062)
    key_weight = scatter_about(splits[6], (DD, DD), DD ** -0.5, 0.21875)
    value_weight = scatter_about(splits[7], (DD, DD), DD ** -0.5, 0.21875)
    out_weight = scatter_about(splits[8], (DD, DD), (2.0 * DD ** -0.5), 0.43164062)
    head_weight = scatter_about(splits[9], (DD, 2 * PP), DD ** -0.5, 0.21875)
    pair_dst = draw_pair_dst(jax.random.fold_in(splits[15], 71), 0)
    pair_count = draw_pair_count(jax.random.fold_in(splits[15], 71), 0)
    depth = scatter_about(splits[12], (IMAGES, L, PP), 0.5, 3.0, ((0, 128),), jnp.float32)
    scale = scatter_about(splits[13], (IMAGES,), 0.5, 3.0, (), jnp.float32)
    focal = scatter_about(splits[14], (IMAGES,), 0.5, 3.0, (), jnp.float32)
    return {"enc_tokens": enc_tokens, "embed_weight": embed_weight, "embed_bias": embed_bias, "query_gain": query_gain, "memory_gain": memory_gain, "query_weight": query_weight, "key_weight": key_weight, "value_weight": value_weight, "out_weight": out_weight, "head_weight": head_weight, "pair_dst": pair_dst, "pair_count": pair_count, "depth": depth, "scale": scale, "focal": focal}


def layer_norm(rows, gain):
    values = rows.astype(jnp.float32)
    center = values - lax.optimization_barrier(jnp.mean(values, axis=-1, keepdims=True))
    spread = lax.optimization_barrier(jnp.mean(center * center, axis=-1, keepdims=True))
    return (center * lax.rsqrt(spread + 1e-05) * gain.astype(jnp.float32)).astype(jnp.bfloat16)

def reference(enc_tokens, embed_weight, embed_bias, query_gain, memory_gain, query_weight, key_weight, value_weight, out_weight, head_weight, pair_dst, pair_count, depth, scale, focal):

    def embed_one(tokens):
        summed = jnp.dot(tokens, embed_weight, preferred_element_type=jnp.float32)
        return (summed + embed_bias.astype(jnp.float32)).astype(jnp.bfloat16)
    embedded = lax.map(embed_one, enc_tokens)

    def prepare(rows):
        normed_q = layer_norm(rows, query_gain)
        normed_m = layer_norm(rows, memory_gain)
        query_rows = jnp.dot(normed_q, query_weight, preferred_element_type=jnp.float32).astype(jnp.bfloat16)
        key_rows = jnp.dot(normed_m, key_weight, preferred_element_type=jnp.float32).astype(jnp.bfloat16)
        value_rows = jnp.dot(normed_m, value_weight, preferred_element_type=jnp.float32).astype(jnp.bfloat16)
        return (query_rows, key_rows, value_rows)
    queries, keys, values = lax.map(prepare, embedded)
    slot_ids = jnp.arange(PAIRS, dtype=jnp.int32)
    owner_ids = (slot_ids // PAIR_CAP).astype(jnp.int32)
    pair_src = (owner_ids * IMG_DEV + slot_ids % IMG_DEV).astype(jnp.int32)

    def one_pair(pair):
        source, target = pair
        query_heads = queries[source].astype(jnp.float32).reshape(L, HEADS, HD)
        key_heads = keys[target].astype(jnp.float32).reshape(L, HEADS, HD)
        value_heads = values[target].astype(jnp.float32).reshape(L, HEADS, HD)
        scores = jnp.einsum('qhd,khd->hqk', query_heads, key_heads) * HD ** (-0.5)
        probs = jax.nn.softmax(scores, axis=-1).astype(jnp.bfloat16)
        mixed = jnp.einsum('hqk,khd->qhd', probs.astype(jnp.float32), value_heads)
        mixed = mixed.astype(jnp.bfloat16).reshape(L, HEADS * HD)
        attended = jnp.dot(mixed, out_weight, preferred_element_type=jnp.float32)
        tokens_out = (embedded[source].astype(jnp.float32) + attended).astype(jnp.bfloat16)
        head = jnp.dot(tokens_out, head_weight, preferred_element_type=jnp.float32)
        return (tokens_out, head[:, :PP], 0.1 + jax.nn.softplus(head[:, PP:]))
    outs, offset, confidence = lax.map(one_pair, (pair_src, pair_dst))
    live = slot_ids % PAIR_CAP < pair_count[owner_ids]
    pair_tokens = jnp.where(live[:, None, None], outs, jnp.zeros_like(outs))
    confidence = jnp.where(live[:, None, None], confidence, jnp.zeros_like(confidence))
    ramp = (2.0 * (jnp.arange(L * PP, dtype=jnp.float32) + 0.5) / (L * PP) - 1.0).reshape(L, PP)
    depth_now, scale_now, focal_now = (depth, scale, focal)
    for turn in range(ITERS):
        shift_terms = scale_now[pair_src] - scale_now[pair_dst]
        focal_terms = focal_now[pair_src] - focal_now[pair_dst]
        resid = depth_now[pair_src] - depth_now[pair_dst] + shift_terms[:, None, None] + focal_terms[:, None, None] * ramp - offset
        weighted = confidence * resid
        depth_grad = jax.ops.segment_sum(weighted, pair_src, IMAGES) - jax.ops.segment_sum(weighted, pair_dst, IMAGES)
        plain = lax.optimization_barrier(jnp.sum(weighted, axis=(1, 2))) / (L * PP)
        slope = lax.optimization_barrier(jnp.sum(weighted * ramp, axis=(1, 2))) / (L * PP)
        scale_grad = jax.ops.segment_sum(plain, pair_src, IMAGES) - jax.ops.segment_sum(plain, pair_dst, IMAGES)
        focal_grad = jax.ops.segment_sum(slope, pair_src, IMAGES) - jax.ops.segment_sum(slope, pair_dst, IMAGES)
        depth_now = depth_now - 0.1 * depth_grad
        scale_now = scale_now - 0.1 * scale_grad
        focal_now = focal_now - 0.1 * focal_grad
    return (pair_tokens, depth_now, scale_now, focal_now)
```

```python
import jax
import jax.numpy as jnp
from jax import lax
from jax.experimental import pallas as pl
from jax.experimental.pallas import tpu as pltpu
from jax.sharding import PartitionSpec as P

HEADS = 12
HEAD = 64
STEP = 0.1
LOG2E = 1.4426950408889634
F32 = jnp.float32
BF16 = jnp.bfloat16


def matmul(a, b, left=1, right=0):
    return lax.dot_general(a, b, (((left,), (right,)), ((), ())), preferred_element_type=F32)


def ramp_of(start, rows, width, total):
    row = lax.broadcasted_iota(jnp.int32, (rows, width), 0) + start
    col = lax.broadcasted_iota(jnp.int32, (rows, width), 1)
    return 2.0 * ((row * width + col).astype(F32) + 0.5) / total - 1.0


def params():
    return pltpu.CompilerParams(vmem_limit_bytes=56 << 20)


def embed_kernel(enc, weight, bias, query_gain, memory_gain, depth, embed, normed_q, packed):
    rows = 256
    width = embed.shape[1]
    for start in range(0, enc.shape[0], rows):
        part = pl.ds(start, rows)
        value = (matmul(enc[part, :], weight[...]) + bias[...]).astype(BF16)
        embed[part, :] = value
        value = value.astype(F32)
        center = value - jnp.mean(value, axis=-1, keepdims=True)
        spread = jnp.mean(center * center, axis=-1, keepdims=True)
        scaled = center * lax.rsqrt(spread + 1e-05)
        normed_q[part, :] = (scaled * query_gain[...]).astype(BF16)
        packed[part, :width] = (scaled * memory_gain[...]).astype(BF16)
        packed[part, width:] = depth[part, :].astype(BF16)


def embed_stage(enc, weight, bias, query_gain, memory_gain, depth):
    tokens, width = enc.shape[0], weight.shape[1]
    return pl.pallas_call(
        embed_kernel,
        out_shape=(
            jax.ShapeDtypeStruct((tokens, width), BF16),
            jax.ShapeDtypeStruct((tokens, width), BF16),
            jax.ShapeDtypeStruct((tokens, width + depth.shape[1]), BF16),
        ),
        compiler_params=params(),
        name="embed_stage",
    )(enc, weight, bias, query_gain, memory_gain, depth)


def attention(query_t, keys, values_t, mixed_t, group):
    tokens = query_t.shape[1]

    def scores(base, half):
        offset = pl.multiple_of(base + half * HEAD, HEAD)
        query = query_t[pl.ds(offset, HEAD), :]
        blank = jnp.zeros_like(query)
        both = jnp.concatenate([query, blank] if half == 0 else [blank, query], axis=0)
        return matmul(keys[:, pl.ds(base, 2 * HEAD)], both), offset

    def finish(score, offset):
        probs = jnp.exp2(score - jnp.max(score, axis=0, keepdims=True)).astype(BF16)
        ones = jnp.ones((16, keys.shape[0]), BF16)
        stacked = jnp.concatenate([values_t[pl.ds(offset, HEAD), :], ones], axis=0)
        mixed = matmul(stacked, probs)
        mixed_t[pl.ds(offset, HEAD), :] = (mixed[:HEAD] * (1.0 / mixed[HEAD : HEAD + 1])).astype(BF16)

    def step(index, carry):
        pending = None
        for pair in range(group):
            base = pl.multiple_of((index * group + pair) * 2 * HEAD, 2 * HEAD)
            for half in range(2):
                current = scores(base, half)
                if pending is not None:
                    finish(*pending)
                pending = current
        finish(*pending)
        return carry

    lax.fori_loop(0, HEADS // 2 // group, step, 0)


def pair_kernel(first, *refs):
    refs = list(refs)
    take = lambda count: [refs.pop(0) for _ in range(count)]
    flags, terms, packed, query_t, embed, key_w, value_wt, out_w, head_w, depth = take(10)
    total_in = None if first else take(1)[0]
    _ = None if first else take(1)[0]
    pair_tokens, sent, total_out = take(3)
    keys, values_t, mixed_t, rows_out, sems = take(5)
    zeros = take(1)[0] if first else None
    tokens, width = embed.shape
    patch = depth.shape[1]
    slots = pair_tokens.shape[0]

    if first:
        zeros[...] = jnp.zeros_like(zeros)
        for slot in range(slots):
            @pl.when(flags[slots + slot] > 0)
            def _():
                pltpu.make_async_copy(zeros, pair_tokens.at[slot], sems.at[slots + slot]).start()

    memory = packed[:, :width]
    keys[...] = matmul(memory, key_w[...]).astype(BF16)
    values_t[...] = matmul(value_wt[...], memory, 1, 1).astype(BF16)
    attention(query_t, keys, values_t, mixed_t, 3)
    rows = 256
    weight = terms[0]
    for start in range(0, tokens, rows):
        part = pl.ds(start, rows)
        attended = matmul(mixed_t[:, part], out_w[...], 0, 0)
        value = (embed[part, :].astype(F32) + attended).astype(BF16)
        rows_out[part, :] = value
        head = matmul(value, head_w[...])
        logit = head[:, patch:]
        soft = jnp.maximum(logit, 0.0) + jnp.log1p(jnp.exp(-jnp.abs(logit)))
        confidence = weight * (0.1 + soft)
        ramp = ramp_of(start, rows, patch, tokens * patch)
        other = packed[part, width:].astype(F32)
        resid = depth[part, :] - other + terms[1] + terms[2] * ramp - head[:, :patch]
        moved = confidence * resid
        sent[0, part, :] = moved.astype(BF16)
        sent[1, part, :] = confidence.astype(BF16)
        total_out[part, :] = moved if first else total_in[part, :] + moved
    for slot in range(slots):
        @pl.when(flags[slot] > 0)
        def _():
            pltpu.make_async_copy(rows_out, pair_tokens.at[slot], sems.at[slot]).start()
    for slot in range(slots):
        @pl.when(flags[slot] > 0)
        def _():
            pltpu.make_async_copy(rows_out, pair_tokens.at[slot], sems.at[slot]).wait()
    if first:
        for slot in range(slots):
            @pl.when(flags[slots + slot] > 0)
            def _():
                pltpu.make_async_copy(zeros, pair_tokens.at[slot], sems.at[slots + slot]).wait()


def pair_stage(flags, terms, packed, query_t, embed, weights, depth, slots, chain):
    first = chain is None
    tokens, width = embed.shape
    patch = depth.shape[1]
    vmem = pl.BlockSpec(memory_space=pltpu.VMEM)
    smem = pl.BlockSpec(memory_space=pltpu.SMEM)
    hbm = pl.BlockSpec(memory_space=pl.ANY)
    operands = [flags, terms, packed, query_t, embed, *weights, depth]
    specs = [smem, smem] + [vmem] * 8
    if not first:
        operands += [chain[1], chain[0]]
        specs += [vmem, hbm]
    scratch = [
        pltpu.VMEM((tokens, width), BF16),
        pltpu.VMEM((width, tokens), BF16),
        pltpu.VMEM((width, tokens), BF16),
        pltpu.VMEM((tokens, width), BF16),
        pltpu.SemaphoreType.DMA((2 * slots,)),
    ]
    if first:
        scratch.append(pltpu.VMEM((tokens, width), BF16))

    def body(*refs):
        pair_kernel(first, *refs)

    return pl.pallas_call(
        body,
        in_specs=specs,
        out_specs=(hbm, vmem, vmem),
        out_shape=(
            jax.ShapeDtypeStruct((slots, tokens, width), BF16),
            jax.ShapeDtypeStruct((2, tokens, patch), BF16),
            jax.ShapeDtypeStruct((tokens, patch), F32),
        ),
        scratch_shapes=scratch,
        input_output_aliases={} if first else {len(operands) - 1: 0},
        compiler_params=params(),
        name="pair_stage",
    )(*operands)


def align_kernel(lanes, pose, depth, total, out_p, out_o, out_x, in_p, in_o, in_x, base, change, poses):
    tokens, patch = depth.shape
    pixels = tokens * patch
    grad = total[...] - in_p[0].astype(F32) - in_o[0].astype(F32) - in_x[0].astype(F32)
    ramp = ramp_of(0, tokens, patch, pixels)
    plain = jnp.sum(grad) / pixels
    slope = jnp.sum(grad * ramp) / pixels
    delta = -STEP * (grad + plain + slope * ramp)
    change[...] = delta.astype(BF16)
    link_p = out_p[1].astype(F32) + in_p[1].astype(F32)
    link_o = out_o[1].astype(F32) + in_o[1].astype(F32)
    back = out_x[1].astype(F32)
    ahead = in_x[1].astype(F32)
    links = (link_p, link_o, back, ahead)
    base[...] = depth[...] - STEP * (2.0 * grad + delta * (link_p + link_o + back + ahead))
    tilted = delta * ramp
    shares = [jnp.sum(link * delta) / pixels for link in links]
    leans = [jnp.sum(link * tilted) / pixels for link in links]
    lane = lax.broadcasted_iota(jnp.int32, (1, poses.shape[1]), 1)

    def spread(start, first, parts):
        own = start - STEP * (2.0 * first + (parts[0] + parts[1] + parts[2] + parts[3]))
        row = jnp.where(lane == lanes[0], own, 0.0)
        for index in range(4):
            row = row + jnp.where(lane == lanes[index + 1], STEP * parts[index], 0.0)
        return row

    poses[0:1, :] = spread(pose[0], plain, shares)
    poses[1:2, :] = spread(pose[1], slope, leans)


def align_stage(lanes, pose, depth, total, outs, ins, images):
    tokens, patch = depth.shape
    vmem = pl.BlockSpec(memory_space=pltpu.VMEM)
    smem = pl.BlockSpec(memory_space=pltpu.SMEM)
    return pl.pallas_call(
        align_kernel,
        in_specs=[smem, smem] + [vmem] * 8,
        out_specs=(vmem, vmem, vmem),
        out_shape=(
            jax.ShapeDtypeStruct((tokens, patch), F32),
            jax.ShapeDtypeStruct((tokens, patch), BF16),
            jax.ShapeDtypeStruct((2, images), F32),
        ),
        compiler_params=params(),
        name="align_stage",
    )(lanes, pose, depth, total, *outs, *ins)


def swap_inner(value, count):
    return lax.ppermute(value, "img", [(i, i ^ 1) for i in range(count)])


def swap_outer(value, count):
    pairs = [(i, i + 1) for i in range(1, count - 1, 2)]
    return lax.ppermute(value, "img", pairs + [(b, a) for a, b in pairs])


def along(value, count, by):
    return lax.ppermute(value, "group", [(i, (i + by) % count) for i in range(count)])


def local(
    enc_tokens,
    embed_weight,
    embed_bias,
    query_gain,
    memory_gain,
    query_weight,
    key_weight,
    value_weight,
    out_weight,
    head_weight,
    pair_dst,
    pair_count,
    depth,
    scale,
    focal,
):
    group_count, img_count = lax.axis_size("group"), lax.axis_size("img")
    group, img = lax.axis_index("group"), lax.axis_index("img")
    slots = pair_dst.shape[0]
    images = scale.shape[0]
    own_id = group * img_count + img
    inner_id = group * img_count + (img ^ 1)
    outer_img = jnp.where(img % 2 == 0, img - 1, img + 1)
    outer_ok = (outer_img >= 0) & (outer_img < img_count)
    outer_id = group * img_count + jnp.clip(outer_img, 0, img_count - 1)
    back_id = (group + group_count - 1) % group_count * img_count + img
    next_id = (group + 1) % group_count * img_count + img
    live = jnp.arange(slots, dtype=jnp.int32) < pair_count[0]
    depth_now = depth[0]

    embed, normed_q, packed = embed_stage(
        enc_tokens[0],
        embed_weight,
        embed_bias[None, :],
        query_gain[None, :],
        memory_gain[None, :],
        depth_now,
    )
    packed_p = swap_inner(packed, img_count)
    packed_x = along(packed, group_count, 1)
    packed_o = swap_outer(packed, img_count)
    query_t = (matmul(query_weight, normed_q, 0, 1) * (HEAD**-0.5 * LOG2E)).astype(BF16)
    weights = (key_weight, value_weight.T, out_weight, head_weight)

    def stage(packed_in, target, chosen, chain):
        hits = live & chosen
        flags = jnp.concatenate([hits, ~live]).astype(jnp.int32)
        shift = scale[own_id] - scale[target]
        tilt = focal[own_id] - focal[target]
        terms = jnp.stack([jnp.sum(hits.astype(F32)), shift, tilt])
        return pair_stage(flags, terms, packed_in, query_t, embed, weights, depth_now, slots, chain)

    to_inner = pair_dst == inner_id
    to_back = pair_dst == back_id
    to_outer = ~to_inner & ~to_back
    tokens_p, sent_p, total_p = stage(packed_p, inner_id, to_inner, None)
    in_p = swap_inner(sent_p, img_count)
    tokens_o, sent_o, total_o = stage(packed_o, outer_id, to_outer, (tokens_p, total_p))
    in_o = swap_outer(sent_o, img_count)
    tokens_x, sent_x, total_x = stage(packed_x, back_id, to_back, (tokens_o, total_o))
    in_x = along(sent_x, group_count, -1)

    lanes = jnp.stack([own_id, inner_id, outer_id, back_id, next_id]).astype(jnp.int32)
    pose = jnp.stack([scale[own_id], focal[own_id]])
    base, change, poses = align_stage(
        lanes, pose, depth_now, total_x, (sent_p, sent_o, sent_x), (in_p, in_o, in_x), images
    )
    change_p = swap_inner(change, img_count)
    change_o = swap_outer(change, img_count)
    change_b = along(change, group_count, 1)
    change_n = along(change, group_count, -1)
    bit = 1
    while bit < img_count:
        poses = poses + lax.ppermute(poses, "img", [(i, i ^ bit) for i in range(img_count)])
        bit *= 2
    bit = 1
    while bit < group_count:
        poses = poses + lax.ppermute(poses, "group", [(i, i ^ bit) for i in range(group_count)])
        bit *= 2
    wide = lambda array: array.astype(F32)
    depth_out = base + STEP * (
        (wide(sent_p[1]) + wide(in_p[1])) * wide(change_p)
        + (wide(sent_o[1]) + wide(in_o[1])) * wide(change_o)
        + wide(sent_x[1]) * wide(change_b)
        + wide(in_x[1]) * wide(change_n)
    )
    return (tokens_x, depth_out[None], poses[0], poses[1])


def solution(mesh):
    placed = (
        P(("group", "img"), None, None),
        P(),
        P(),
        P(),
        P(),
        P(),
        P(),
        P(),
        P(),
        P(),
        P(("group", "img")),
        P(("group", "img")),
        P(("group", "img"), None, None),
        P(),
        P(),
    )
    return jax.shard_map(
        local,
        mesh=mesh,
        in_specs=placed,
        out_specs=(P(("group", "img"), None, None), P(("group", "img"), None, None), P(), P()),
        check_vma=False,
    )
```

```python
import jax
import jax.numpy as jnp
from jax import lax
from jax.experimental import pallas as pl
from jax.experimental.pallas import tpu as pltpu
from jax.sharding import PartitionSpec as P

HEADS = 12
HEAD = 64
STEP = 0.1
LOG2E = 1.4426950408889634
F32 = jnp.float32
BF16 = jnp.bfloat16


def matmul(a, b, left=1, right=0):
    return lax.dot_general(a, b, (((left,), (right,)), ((), ())), preferred_element_type=F32)


def ramp_of(start, rows, width, total):
    row = lax.broadcasted_iota(jnp.int32, (rows, width), 0) + start
    col = lax.broadcasted_iota(jnp.int32, (rows, width), 1)
    return 2.0 * ((row * width + col).astype(F32) + 0.5) / total - 1.0


def params():
    return pltpu.CompilerParams(vmem_limit_bytes=24 << 20)


VMEM = pl.BlockSpec(memory_space=pltpu.VMEM)
SMEM = pl.BlockSpec(memory_space=pltpu.SMEM)
HBM = pl.BlockSpec(memory_space=pl.ANY)


def neighbours():
    group_count, img_count = lax.axis_size("group"), lax.axis_size("img")
    group, img = lax.axis_index("group"), lax.axis_index("img")
    base = group * img_count
    inner = base + img + 1 - 2 * (img % 2)
    outer = base + jnp.clip(img - 1 + 2 * (img % 2), 0, img_count - 1)
    back = (group + group_count - 1) % group_count * img_count + img
    ahead = (group + 1) % group_count * img_count + img
    return base + img, inner, outer, back, ahead


def normed(value, gain):
    value = value.astype(F32)
    center = value - jnp.mean(value, axis=-1, keepdims=True)
    spread = jnp.mean(center * center, axis=-1, keepdims=True)
    return (center * lax.rsqrt(spread + 1e-05) * gain).astype(BF16)


def embed_kernel(enc, weight, bias, memory_gain, depth, embed, packed):
    width = embed.shape[1]
    value = (matmul(enc[...], weight[...]) + bias[...][None, :]).astype(BF16)
    embed[...] = value
    packed[:, :width] = normed(value, memory_gain[...][None, :])
    packed[:, width:] = depth[...].astype(BF16)


def embed_stage(enc, weight, bias, memory_gain, depth):
    tokens, width = enc.shape[0], weight.shape[1]
    patch = depth.shape[1]
    rows = 256
    whole = lambda array: pl.BlockSpec(array.shape, lambda i: (0,) * array.ndim)
    strip = lambda cols: pl.BlockSpec((rows, cols), lambda i: (i, 0))
    return pl.pallas_call(
        embed_kernel,
        grid=(tokens // rows,),
        in_specs=[strip(enc.shape[1]), whole(weight), whole(bias), whole(memory_gain), strip(patch)],
        out_specs=(strip(width), strip(width + patch)),
        out_shape=(
            jax.ShapeDtypeStruct((tokens, width), BF16),
            jax.ShapeDtypeStruct((tokens, width + patch), BF16),
        ),
        compiler_params=params(),
        name="embed_stage",
    )(enc, weight, bias, memory_gain, depth)


def query_kernel(embed, gain, query_w, value_w, query_t, value_wt):
    scaled = HEAD**-0.5 * LOG2E
    value_wt[...] = value_w[...].T
    rows = 256
    for start in range(0, embed.shape[0], rows):
        part = pl.ds(start, rows)
        value = normed(embed[part, :], gain[...][None, :])
        query_t[:, part] = (matmul(query_w[...], value, 0, 1) * scaled).astype(BF16)


def query_stage(embed, gain, query_w, value_w):
    return pl.pallas_call(
        query_kernel,
        in_specs=[VMEM] * 4,
        out_specs=(VMEM, VMEM),
        out_shape=(
            jax.ShapeDtypeStruct(embed.shape[::-1], BF16),
            jax.ShapeDtypeStruct(value_w.shape[::-1], BF16),
        ),
        compiler_params=params(),
        name="query_stage",
    )(embed, gain, query_w, value_w)


def attention(query_t, keys, values_t, mixed_t, first, count, group):
    def scores(base, half):
        offset = pl.multiple_of(base + half * HEAD, HEAD)
        query = query_t[pl.ds(offset, HEAD), pl.ds(first, count)]
        blank = jnp.zeros_like(query)
        both = jnp.concatenate([query, blank] if half == 0 else [blank, query], axis=0)
        return matmul(keys[:, pl.ds(base, 2 * HEAD)], both), offset

    def finish(score, offset):
        probs = jnp.exp2(score - jnp.max(score, axis=0, keepdims=True)).astype(BF16)
        ones = jnp.ones((16, keys.shape[0]), BF16)
        stacked = jnp.concatenate([values_t[pl.ds(offset, HEAD), :], ones], axis=0)
        mixed = matmul(stacked, probs)
        mixed_t[pl.ds(offset, HEAD), :] = (mixed[:HEAD] * (1.0 / mixed[HEAD : HEAD + 1])).astype(BF16)

    def step(index, carry):
        pending = None
        for pair in range(group):
            base = pl.multiple_of((index * group + pair) * 2 * HEAD, 2 * HEAD)
            for half in range(2):
                current = scores(base, half)
                if pending is not None:
                    finish(*pending)
                pending = current
        finish(*pending)
        return carry

    lax.fori_loop(0, HEADS // 2 // group, step, 0)


def pair_kernel(which, first, count, make, chained, *refs):
    refs = list(refs)

    def take(number):
        return [refs.pop(0) for _ in range(number)]

    dst, live, scale, focal, query_t, embed, out_w, head_w, depth, packed = take(10)
    keys, values_t, key_w, value_wt, total_in = None, None, None, None, None
    if make:
        key_w, value_wt = take(2)
    else:
        keys, values_t = take(2)
    if chained:
        total_in = take(2)[0]
    pair_tokens, sent, total_out = take(3)
    if make:
        keys, values_t = take(2)
    mixed_t, rows_out, sems = take(3)
    zeros = None if chained else take(1)[0]
    tokens, width = embed.shape
    patch = depth.shape[1]
    slots = pair_tokens.shape[0]
    ids = neighbours()
    own, target = ids[0], ids[which]
    hits = [(dst[slot] == target) & (slot < live[0]) for slot in range(slots)]
    dead = [slot >= live[0] for slot in range(slots)]

    def clear(slot):
        return pltpu.make_async_copy(zeros, pair_tokens.at[slot], sems.at[slots + slot])

    def write(slot):
        place = pair_tokens.at[slot, pl.ds(first, count)]
        return pltpu.make_async_copy(rows_out, place, sems.at[slot])

    if not chained:
        zeros[...] = jnp.zeros_like(zeros)
        for slot in range(slots):
            pl.when(dead[slot])(lambda slot=slot: clear(slot).start())
    if make:
        memory = packed[:, :width]
        keys[...] = matmul(memory, key_w[...]).astype(BF16)
        values_t[...] = matmul(value_wt[...], memory, 1, 1).astype(BF16)
    attention(query_t, keys, values_t, mixed_t, first, count, 3)
    rows = 256 if count % 256 == 0 else 128
    weight = jnp.float32(0.0)
    for slot in range(slots):
        weight = weight + jnp.where(hits[slot], 1.0, 0.0)
    shift = scale[own] - scale[target]
    tilt = focal[own] - focal[target]
    for start in range(0, count, rows):
        part = pl.ds(start, rows)
        whole = pl.ds(first + start, rows)
        attended = matmul(mixed_t[:, part], out_w[...], 0, 0)
        value = (embed[whole, :].astype(F32) + attended).astype(BF16)
        rows_out[part, :] = value
        head = matmul(value, head_w[...])
        logit = head[:, patch:]
        soft = jnp.maximum(logit, 0.0) + jnp.log1p(jnp.exp(-jnp.abs(logit)))
        confidence = weight * (0.1 + soft)
        ramp = ramp_of(first + start, rows, patch, tokens * patch)
        other = packed[whole, width:].astype(F32)
        resid = depth[whole, :] - other + shift + tilt * ramp - head[:, :patch]
        moved = confidence * resid
        sent[0, part, :] = moved.astype(BF16)
        sent[1, part, :] = confidence.astype(BF16)
        total_out[part, :] = total_in[whole, :] + moved if chained else moved
    for slot in range(slots):
        pl.when(hits[slot])(lambda slot=slot: write(slot).start())
    for slot in range(slots):
        pl.when(hits[slot])(lambda slot=slot: write(slot).wait())
    if not chained:
        for slot in range(slots):
            pl.when(dead[slot])(lambda slot=slot: clear(slot).wait())


def pair_stage(which, first, count, common, packed, weights, chain, made=None, keep=False):
    tokens, width = common[5].shape
    patch = common[8].shape[1]
    slots = common[0].shape[0]
    make, chained = made is None, chain is not None
    operands = [*common, packed, *(weights if make else made)]
    specs = [SMEM] * 4 + [VMEM] * 8
    if chained:
        operands += [chain[1], chain[0]]
        specs += [VMEM, HBM]
    kept = [jax.ShapeDtypeStruct((tokens, width), BF16), jax.ShapeDtypeStruct((width, tokens), BF16)]
    scratch = [] if keep or not make else [pltpu.VMEM((tokens, width), BF16), pltpu.VMEM((width, tokens), BF16)]
    scratch += [
        pltpu.VMEM((width, count), BF16),
        pltpu.VMEM((count, width), BF16),
        pltpu.SemaphoreType.DMA((2 * slots,)),
    ]
    if not chained:
        scratch.append(pltpu.VMEM((tokens, width), BF16))

    def body(*refs):
        pair_kernel(which, first, count, make, chained, *refs)

    return pl.pallas_call(
        body,
        in_specs=specs,
        out_specs=(HBM, VMEM, VMEM) + ((VMEM, VMEM) if keep else ()),
        out_shape=(
            jax.ShapeDtypeStruct((slots, tokens, width), BF16),
            jax.ShapeDtypeStruct((2, count, patch), BF16),
            jax.ShapeDtypeStruct((count, patch), F32),
        )
        + (tuple(kept) if keep else ()),
        scratch_shapes=scratch,
        input_output_aliases={len(operands) - 1: 0} if chained else {},
        compiler_params=params(),
    )(*operands)


def align_kernel(scale, focal, depth, *refs):
    totals, out_x, in_x = refs[0:2], refs[2:4], refs[4:6]
    out_p, out_o, in_p, in_o = refs[6:10]
    base, change, poses, grads = refs[10:]
    tokens, patch = depth.shape
    pixels = tokens * patch
    rows = 64
    half = tokens // 2

    def wide(ref, index, start):
        return ref[index, pl.ds(start, rows), :].astype(F32)

    def fold(value):
        return jnp.sum(value.reshape(rows // 8, 8, patch), axis=0)

    plain = jnp.zeros((8, patch), F32)
    slope = jnp.zeros((8, patch), F32)
    for start in range(0, tokens, rows):
        piece, local_start = start // half, start % half
        grad = totals[piece][pl.ds(local_start, rows), :] - wide(in_x[piece], 0, local_start)
        grad = grad - wide(in_p, 0, start) - wide(in_o, 0, start)
        grads[pl.ds(start, rows), :] = grad
        plain = plain + fold(grad)
        slope = slope + fold(grad * ramp_of(start, rows, patch, pixels))
    plain = jnp.sum(plain) / pixels
    slope = jnp.sum(slope) / pixels
    sums = [jnp.zeros((8, patch), F32) for _ in range(8)]
    for start in range(0, tokens, rows):
        part = pl.ds(start, rows)
        piece, local_start = start // half, start % half
        grad = grads[part, :]
        ramp = ramp_of(start, rows, patch, pixels)
        delta = -STEP * (grad + plain + slope * ramp)
        change[part, :] = delta.astype(BF16)
        links = [
            wide(out_p, 1, start) + wide(in_p, 1, start),
            wide(out_o, 1, start) + wide(in_o, 1, start),
            wide(out_x[piece], 1, local_start),
            wide(in_x[piece], 1, local_start),
        ]
        shares = [link * delta for link in links]
        base[part, :] = depth[part, :] - STEP * (
            2.0 * grad + (shares[0] + shares[1] + shares[2] + shares[3])
        )
        for index in range(4):
            sums[index] = sums[index] + fold(shares[index])
            sums[index + 4] = sums[index + 4] + fold(shares[index] * ramp)
    sums = [jnp.sum(value) / pixels for value in sums]
    ids = neighbours()
    lane = lax.broadcasted_iota(jnp.int32, (1, poses.shape[1]), 1)

    def spread(start, first, parts):
        own = start - STEP * (2.0 * first + (parts[0] + parts[1] + parts[2] + parts[3]))
        row = jnp.where(lane == ids[0], own, 0.0)
        for index in range(4):
            row = row + jnp.where(lane == ids[index + 1], STEP * parts[index], 0.0)
        return row

    poses[0:1, :] = spread(scale[ids[0]], plain, sums[:4])
    poses[1:2, :] = spread(focal[ids[0]], slope, sums[4:])


def align_stage(scale, focal, depth, totals, out_x, in_x, outs, ins):
    tokens, patch = depth.shape
    return pl.pallas_call(
        align_kernel,
        in_specs=[SMEM, SMEM] + [VMEM] * 11,
        out_specs=(VMEM, VMEM, VMEM),
        out_shape=(
            jax.ShapeDtypeStruct((tokens, patch), F32),
            jax.ShapeDtypeStruct((tokens, patch), BF16),
            jax.ShapeDtypeStruct((2, scale.shape[0]), F32),
        ),
        scratch_shapes=[pltpu.VMEM((tokens, patch), F32)],
        compiler_params=params(),
        name="align_stage",
    )(scale, focal, depth, *totals, *out_x, *in_x, *outs, *ins)


def final_kernel(base, *refs):
    out_x, in_x = refs[0:2], refs[2:4]
    out_p, out_o, in_p, in_o, change_p, change_o, change_b, change_n, result = refs[4:]
    tokens, _ = base.shape
    rows = 64
    half = tokens // 2

    def wide(ref, index, start):
        return ref[index, pl.ds(start, rows), :].astype(F32)

    for start in range(0, tokens, rows):
        part = pl.ds(start, rows)
        piece, local_start = start // half, start % half
        step = (wide(out_p, 1, start) + wide(in_p, 1, start)) * change_p[part, :].astype(F32)
        step += (wide(out_o, 1, start) + wide(in_o, 1, start)) * change_o[part, :].astype(F32)
        step += wide(out_x[piece], 1, local_start) * change_b[part, :].astype(F32)
        step += wide(in_x[piece], 1, local_start) * change_n[part, :].astype(F32)
        result[part, :] = base[part, :] + STEP * step


def final_stage(base, out_x, in_x, outs, ins, changes):
    return pl.pallas_call(
        final_kernel,
        in_specs=[VMEM] * 13,
        out_specs=VMEM,
        out_shape=jax.ShapeDtypeStruct(base.shape, F32),
        compiler_params=params(),
        name="final_stage",
    )(base, *out_x, *in_x, *outs, *ins, *changes)


def swap_inner(value):
    return lax.ppermute(value, "img", [(i, i ^ 1) for i in range(lax.axis_size("img"))])


def swap_outer(value):
    pairs = [(i, i + 1) for i in range(1, lax.axis_size("img") - 1, 2)]
    return lax.ppermute(value, "img", pairs + [(b, a) for a, b in pairs])


def along(value, by):
    count = lax.axis_size("group")
    return lax.ppermute(value, "group", [(i, (i + by) % count) for i in range(count)])


def local(
    enc_tokens,
    embed_weight,
    embed_bias,
    query_gain,
    memory_gain,
    query_weight,
    key_weight,
    value_weight,
    out_weight,
    head_weight,
    pair_dst,
    pair_count,
    depth,
    scale,
    focal,
):
    tokens = enc_tokens.shape[1]
    half = tokens // 2
    depth_now = depth[0]
    embed, packed = embed_stage(enc_tokens[0], embed_weight, embed_bias, memory_gain, depth_now)
    packed_x = along(packed, 1)
    packed_o = swap_outer(packed)
    packed_p = swap_inner(packed)
    query_t, value_wt = query_stage(embed, query_gain, query_weight, value_weight)
    common = (pair_dst, pair_count, scale, focal, query_t, embed, out_weight, head_weight, depth_now)
    weights = (key_weight, value_wt)
    tokens_p, sent_p, total_p = pair_stage(1, 0, tokens, common, packed_p, weights, None)
    in_p = swap_inner(sent_p)
    tokens_o, sent_o, total_o = pair_stage(
        2, 0, tokens, common, packed_o, weights, (tokens_p, total_p)
    )
    in_o = swap_outer(sent_o)
    tokens_a, sent_a, total_a, *made = pair_stage(
        3, 0, half, common, packed_x, weights, (tokens_o, total_o), keep=True
    )
    in_a = along(sent_a, -1)
    tokens_b, sent_b, total_b = pair_stage(
        3, half, half, common, packed_x, weights, (tokens_a, total_o), made=made
    )
    in_b = along(sent_b, -1)
    out_x, in_x, outs, ins = (sent_a, sent_b), (in_a, in_b), (sent_p, sent_o), (in_p, in_o)
    base, change, poses = align_stage(scale, focal, depth_now, (total_a, total_b), out_x, in_x, outs, ins)
    changes = (swap_inner(change), swap_outer(change), along(change, 1), along(change, -1))
    for axis, masks in (("img", (1, 2, 6, 8, 24)), ("group", (1, 3))):
        for mask in masks:
            pairs = [(i, i ^ mask) for i in range(lax.axis_size(axis))]
            poses = poses + lax.ppermute(poses, axis, pairs)
    depth_out = final_stage(base, out_x, in_x, outs, ins, changes)
    return (tokens_b, depth_out[None], poses[0], poses[1])


def solution(mesh):
    whole = P(("group", "img"), None, None)
    line = P(("group", "img"))
    return jax.shard_map(
        local,
        mesh=mesh,
        in_specs=(whole, *[P()] * 9, line, line, whole, P(), P()),
        out_specs=(whole, whole, P(), P()),
        check_vma=False,
    )
```

```python
import jax
import jax.numpy as jnp
from jax import lax
from jax.experimental import pallas as pl
from jax.experimental.pallas import tpu as pltpu
from jax.sharding import PartitionSpec as P

HEADS = 12
HEAD = 64
STEP = 0.1
FAST = 3
LOG2E = 1.4426950408889634
F32 = jnp.float32
BF16 = jnp.bfloat16


def matmul(a, b, left=1, right=0):
    return lax.dot_general(a, b, (((left,), (right,)), ((), ())), preferred_element_type=F32)


def ramp_of(start, rows, width, total):
    row = lax.broadcasted_iota(jnp.int32, (rows, width), 0) + start
    col = lax.broadcasted_iota(jnp.int32, (rows, width), 1)
    return 2.0 * ((row * width + col).astype(F32) + 0.5) / total - 1.0


def params(mebi=24):
    return pltpu.CompilerParams(vmem_limit_bytes=mebi << 20)


VMEM = pl.BlockSpec(memory_space=pltpu.VMEM)
SMEM = pl.BlockSpec(memory_space=pltpu.SMEM)
HBM = pl.BlockSpec(memory_space=pl.ANY)


def neighbours():
    group_count, img_count = lax.axis_size("group"), lax.axis_size("img")
    group, img = lax.axis_index("group"), lax.axis_index("img")
    base = group * img_count
    inner = base + img + 1 - 2 * (img % 2)
    outer = base + jnp.clip(img - 1 + 2 * (img % 2), 0, img_count - 1)
    back = (group + group_count - 1) % group_count * img_count + img
    ahead = (group + 1) % group_count * img_count + img
    return base + img, inner, outer, back, ahead


def normed(value, gain):
    value = value.astype(F32)
    center = value - jnp.mean(value, axis=-1, keepdims=True)
    spread = jnp.mean(center * center, axis=-1, keepdims=True)
    return (center * lax.rsqrt(spread + 1e-05) * gain).astype(BF16)


def embed_kernel(enc, weight, bias, memory_gain, depth, embed, rows_out, late, *scratch):
    enc_v, weight_v, depth_v, embed_v, rows_v, late_v, arrive, leave = scratch
    tokens = embed.shape[0]
    count = 3
    rows = tokens // count
    moves = [pltpu.make_async_copy(weight, weight_v, arrive.at[0])]
    for index in range(count):
        part = pl.ds(index * rows, rows)
        moves.append(pltpu.make_async_copy(enc.at[part], enc_v.at[part], arrive.at[index + 1]))
    moves.append(pltpu.make_async_copy(depth, depth_v, arrive.at[count + 1]))
    for move in moves:
        move.start()
    moves[0].wait()
    out = []
    for index in range(count):
        part = pl.ds(index * rows, rows)
        moves[index + 1].wait()
        value = (matmul(enc_v[part, :], weight_v[...]) + bias[...][None, :]).astype(BF16)
        embed_v[part, :] = value
        rows_v[part, :] = normed(value, memory_gain[...][None, :])
        for place, (source, target) in enumerate(((rows_v, rows_out), (embed_v, embed))):
            out.append(pltpu.make_async_copy(source.at[part], target.at[part], leave.at[index * 2 + place]))
            out[-1].start()
    moves[-1].wait()
    late_v[...] = depth_v[...].astype(BF16)
    out.append(pltpu.make_async_copy(late_v, late, leave.at[count * 2]))
    out[-1].start()
    for move in out:
        move.wait()


def embed_stage(enc, weight, bias, memory_gain, depth):
    tokens, width = enc.shape[0], weight.shape[1]
    patch = depth.shape[1]
    shapes = [(tokens, width), (tokens, width), (tokens, patch)]
    return pl.pallas_call(
        embed_kernel,
        in_specs=[HBM, HBM, VMEM, VMEM, HBM],
        out_specs=(HBM,) * 3,
        out_shape=tuple(jax.ShapeDtypeStruct(shape, BF16) for shape in shapes),
        scratch_shapes=[
            pltpu.VMEM(enc.shape, BF16),
            pltpu.VMEM(weight.shape, BF16),
            pltpu.VMEM(depth.shape, F32),
            *[pltpu.VMEM(shape, BF16) for shape in shapes],
            pltpu.SemaphoreType.DMA((5,)),
            pltpu.SemaphoreType.DMA((7,)),
        ],
        compiler_params=params(60),
        name="embed_stage",
    )(enc, weight, bias, memory_gain, depth)


def query_kernel(embed, gain, query_w, value_w, query_t, value_wt, peak):
    scaled = HEAD**-0.5 * LOG2E
    value_wt[...] = value_w[...].T
    rows = 256
    largest = jnp.float32(0.0)
    for start in range(0, embed.shape[0], rows):
        part = pl.ds(start, rows)
        value = normed(embed[part, :], gain[...][None, :])
        query = (matmul(query_w[...], value, 0, 1) * scaled).astype(BF16)
        query_t[:, part] = query
        query = query.astype(F32)
        norm = jnp.sum((query * query).reshape(HEADS, HEAD, rows), axis=1)
        largest = jnp.maximum(largest, jnp.max(norm))
    peak[...] = jnp.full(peak.shape, largest, F32)


def query_stage(embed, gain, query_w, value_w):
    return pl.pallas_call(
        query_kernel,
        in_specs=[VMEM] * 4,
        out_specs=(VMEM,) * 3,
        out_shape=(
            jax.ShapeDtypeStruct(embed.shape[::-1], BF16),
            jax.ShapeDtypeStruct(value_w.shape[::-1], BF16),
            jax.ShapeDtypeStruct((8, 128), F32),
        ),
        compiler_params=params(),
        name="query_stage",
    )(embed, gain, query_w, value_w)


def attention(query_t, keys, values_t, mixed_t, first, count, group, shifted):
    def scores(base, half):
        offset = pl.multiple_of(base + half * HEAD, HEAD)
        query = query_t[pl.ds(offset, HEAD), pl.ds(first, count)]
        blank = jnp.zeros_like(query)
        both = jnp.concatenate([query, blank] if half == 0 else [blank, query], axis=0)
        return matmul(keys[:, pl.ds(base, 2 * HEAD)], both), offset

    def finish(score, offset):
        if shifted:
            score = score - jnp.max(score, axis=0, keepdims=True)
        probs = jnp.exp2(score).astype(BF16)
        ones = jnp.ones((16, keys.shape[0]), BF16)
        stacked = jnp.concatenate([values_t[pl.ds(offset, HEAD), :], ones], axis=0)
        mixed = matmul(stacked, probs)
        mixed_t[pl.ds(offset, HEAD), :] = (mixed[:HEAD] * (1.0 / mixed[HEAD : HEAD + 1])).astype(BF16)

    def single(head, carry):
        base = pl.multiple_of(head // 2 * 2 * HEAD, 2 * HEAD)
        both = query_t[pl.ds(base, 2 * HEAD), pl.ds(first, count)]
        row = lax.broadcasted_iota(jnp.int32, both.shape, 0) // HEAD
        both = jnp.where(row == head % 2, both, jnp.zeros_like(both))
        finish(matmul(keys[:, pl.ds(base, 2 * HEAD)], both), pl.multiple_of(head * HEAD, HEAD))
        return carry

    def step(index, carry):
        pending = None
        for pair in range(group):
            base = pl.multiple_of((index * group + pair) * 2 * HEAD, 2 * HEAD)
            for half in range(2):
                current = scores(base, half)
                if pending is not None:
                    finish(*pending)
                pending = current
        finish(*pending)
        return carry

    if shifted:
        lax.fori_loop(0, HEADS, single, 0)
    else:
        lax.fori_loop(0, HEADS // 2 // group, step, 0)


def key_peak(keys):
    width = keys.shape[1]
    square = keys[...].astype(F32)
    square = (square * square).astype(BF16)
    row = lax.broadcasted_iota(jnp.int32, (width, 128), 0) // HEAD
    col = lax.broadcasted_iota(jnp.int32, (width, 128), 1)
    return jnp.max(matmul(square, jnp.where(row == col, 1.0, 0.0).astype(BF16)))


def pair_kernel(which, first, count, make, keep, chained, *refs):
    refs = list(refs)

    def take(number):
        return [refs.pop(0) for _ in range(number)]

    dst, live, scale, focal, query_t, peak, embed, out_w, head_w, depth = take(10)
    if make:
        packed, key_w, value_wt = take(3)
    else:
        keys, values_t, reach = take(3)
    if chained:
        take(1)
    pair_tokens, sent, moved_out = take(3)
    if make:
        keys, values_t = take(2)
        reach = take(1)[0] if keep else None
    mixed_t, rows_out, sems = take(3)
    zeros = None if chained else take(1)[0]
    tokens, _ = embed.shape
    patch = depth.shape[1]
    slots = pair_tokens.shape[0]
    ids = neighbours()
    own, target = ids[0], ids[which]
    hits = [(dst[slot] == target) & (slot < live[0]) for slot in range(slots)]
    dead = [slot >= live[0] for slot in range(slots)]

    def clear(slot):
        return pltpu.make_async_copy(zeros, pair_tokens.at[slot], sems.at[slots + slot])

    def write(slot):
        place = pair_tokens.at[slot, pl.ds(first, count)]
        return pltpu.make_async_copy(rows_out, place, sems.at[slot])

    if not chained:
        zeros[...] = jnp.zeros_like(zeros)
        for slot in range(slots):
            pl.when(dead[slot])(lambda slot=slot: clear(slot).start())
    if make:
        memory = packed[...]
        keys[...] = matmul(memory, key_w[...]).astype(BF16)
        values_t[...] = matmul(value_wt[...], memory, 1, 1).astype(BF16)
        largest = key_peak(keys)
        if keep:
            reach[...] = jnp.full(reach.shape, largest, F32)
    else:
        largest = jnp.max(reach[...])
    small = jnp.max(peak[...]) * largest <= 8000.0

    @pl.when(small)
    def _():
        attention(query_t, keys, values_t, mixed_t, first, count, FAST, False)

    @pl.when(jnp.logical_not(small))
    def _():
        attention(query_t, keys, values_t, mixed_t, first, count, 1, True)

    rows = 256 if count % 256 == 0 else 128
    weight = jnp.float32(0.0)
    for slot in range(slots):
        weight = weight + jnp.where(hits[slot], 1.0, 0.0)
    shift = scale[own] - scale[target]
    tilt = focal[own] - focal[target]
    for start in range(0, count, rows):
        part = pl.ds(start, rows)
        whole = pl.ds(first + start, rows)
        attended = matmul(mixed_t[:, part], out_w[...], 0, 0)
        value = (embed[whole, :].astype(F32) + attended).astype(BF16)
        rows_out[part, :] = value
        head = matmul(value, head_w[...])
        logit = head[:, patch:]
        soft = jnp.maximum(logit, 0.0) + jnp.log1p(jnp.exp(-jnp.abs(logit)))
        confidence = weight * (0.1 + soft)
        ramp = ramp_of(first + start, rows, patch, tokens * patch)
        moved = confidence * (depth[whole, :] + shift + tilt * ramp - head[:, :patch])
        sent[0, part, :] = moved.astype(BF16)
        sent[1, part, :] = confidence.astype(BF16)
        moved_out[part, :] = moved
        if sent.shape[0] == 3:
            sent[2, part, :] = depth[whole, :].astype(BF16)
    for slot in range(slots):
        pl.when(hits[slot])(lambda slot=slot: write(slot).start())
    for slot in range(slots):
        pl.when(hits[slot])(lambda slot=slot: write(slot).wait())
    if not chained:
        for slot in range(slots):
            pl.when(dead[slot])(lambda slot=slot: clear(slot).wait())


def pair_stage(which, first, count, common, source, chain=None, keep=False):
    tokens, width = common[6].shape
    patch = common[9].shape[1]
    slots = common[0].shape[0]
    chained = chain is not None
    make = source[0].shape[0] == tokens and source[2].shape == (width, width)
    operands = [*common, *source]
    specs = [SMEM] * 4 + [VMEM] * (len(operands) - 4)
    if chained:
        operands.append(chain)
        specs.append(HBM)
    kept = ((tokens, width), (width, tokens))
    scratch = [] if keep or not make else [pltpu.VMEM(shape, BF16) for shape in kept]
    scratch += [
        pltpu.VMEM((width, count), BF16),
        pltpu.VMEM((count, width), BF16),
        pltpu.SemaphoreType.DMA((2 * slots,)),
    ]
    if not chained:
        scratch.append(pltpu.VMEM((tokens, width), BF16))
    results = [
        jax.ShapeDtypeStruct((slots, tokens, width), BF16),
        jax.ShapeDtypeStruct((2 if which == 3 else 3, count, patch), BF16),
        jax.ShapeDtypeStruct((count, patch), F32),
    ]
    if keep:
        results += [jax.ShapeDtypeStruct(shape, BF16) for shape in kept]
        results.append(jax.ShapeDtypeStruct((8, 128), F32))

    def body(*refs):
        pair_kernel(which, first, count, make, keep, chained, *refs)

    return pl.pallas_call(
        body,
        in_specs=specs,
        out_specs=(HBM,) + (VMEM,) * (len(results) - 1),
        out_shape=tuple(results),
        scratch_shapes=scratch,
        input_output_aliases={len(operands) - 1: 0} if chained else {},
        compiler_params=params(),
    )(*operands)


def strip(pieces, start, rows, *index):
    for piece in pieces:
        height = piece.shape[-2]
        if start < height:
            return piece[(*index, pl.ds(start, rows), slice(None))].astype(F32)
        start -= height


def wide(pieces, index, start, rows):
    return strip(pieces, start, rows, index)


def align_kernel(scale, focal, depth, *refs):
    moved_x, (moved_o, moved_p), out_x, in_x = [refs[2 * index : 2 * index + 2] for index in range(4)]
    moved_o, moved_p = (moved_o,), (moved_p,)
    out_o, in_o, out_p, in_p, late = [refs[index : index + 1] for index in range(8, 13)]
    base, change, poses, grads = refs[13:]
    tokens, patch = depth.shape
    pixels = tokens * patch
    rows = 64

    def fold(value):
        return jnp.sum(value.reshape(rows // 8, 8, patch), axis=0)

    plain = jnp.zeros((8, patch), F32)
    slope = jnp.zeros((8, patch), F32)
    for start in range(0, tokens, rows):
        own = depth[pl.ds(start, rows), :]
        grad = jnp.zeros_like(own)
        for pieces in (moved_x, moved_o, moved_p):
            grad = grad + strip(pieces, start, rows)
        for pieces in (in_x, in_o, in_p):
            grad = grad - wide(pieces, 0, start, rows) + wide(pieces, 1, start, rows) * own
        others = (strip(late, start, rows), wide(in_o, 2, start, rows), wide(in_p, 2, start, rows))
        for pieces, other in zip((out_x, out_o, out_p), others):
            grad = grad - wide(pieces, 1, start, rows) * other
        grads[pl.ds(start, rows), :] = grad
        plain = plain + fold(grad)
        slope = slope + fold(grad * ramp_of(start, rows, patch, pixels))
    plain = jnp.sum(plain) / pixels
    slope = jnp.sum(slope) / pixels
    sums = [jnp.zeros((8, patch), F32) for _ in range(8)]
    for start in range(0, tokens, rows):
        part = pl.ds(start, rows)
        grad = grads[part, :]
        ramp = ramp_of(start, rows, patch, pixels)
        delta = -STEP * (grad + plain + slope * ramp)
        change[part, :] = delta.astype(BF16)
        links = [
            wide(out_p, 1, start, rows) + wide(in_p, 1, start, rows),
            wide(out_o, 1, start, rows) + wide(in_o, 1, start, rows),
            wide(out_x, 1, start, rows),
            wide(in_x, 1, start, rows),
        ]
        shares = [link * delta for link in links]
        base[part, :] = depth[part, :] - STEP * (
            2.0 * grad + (shares[0] + shares[1] + shares[2] + shares[3])
        )
        for index in range(4):
            sums[index] = sums[index] + fold(shares[index])
            sums[index + 4] = sums[index + 4] + fold(shares[index] * ramp)
    sums = [jnp.sum(value) / pixels for value in sums]
    ids = neighbours()
    lane = lax.broadcasted_iota(jnp.int32, (1, poses.shape[0]), 1)

    def spread(start, first, parts):
        own = start - STEP * (2.0 * first + (parts[0] + parts[1] + parts[2] + parts[3]))
        row = jnp.where(lane == ids[0], own, 0.0)
        for index in range(4):
            row = row + jnp.where(lane == ids[index + 1], STEP * parts[index], 0.0)
        return row

    images = lane.shape[1]
    for half, row in enumerate((spread(scale[ids[0]], plain, sums[:4]), spread(focal[ids[0]], slope, sums[4:]))):
        place = slice(half * images, (half + 1) * images)
        poses[:, :, place] = jnp.broadcast_to(row[None], (images, 1, images))


def align_stage(scale, focal, depth, *arrays):
    tokens, patch = depth.shape
    return pl.pallas_call(
        align_kernel,
        in_specs=[SMEM, SMEM] + [VMEM] * (len(arrays) + 1),
        out_specs=(VMEM, VMEM, VMEM),
        out_shape=(
            jax.ShapeDtypeStruct((tokens, patch), F32),
            jax.ShapeDtypeStruct((tokens, patch), BF16),
            jax.ShapeDtypeStruct((scale.shape[0], 1, 2 * scale.shape[0]), F32),
        ),
        scratch_shapes=[pltpu.VMEM((tokens, patch), F32)],
        compiler_params=params(),
        name="align_stage",
    )(scale, focal, depth, *arrays)


def final_kernel(base, *refs):
    out_x, in_x = refs[0:2], refs[2:4]
    out_o, in_o, out_p, in_p = [refs[index : index + 1] for index in range(4, 8)]
    change_p, change_o, change_b, change_n, poses, result, pose = refs[8:]
    images = poses.shape[0]
    pose[0:1, :] = jnp.sum(poses[:, :, :images], axis=0)
    pose[1:2, :] = jnp.sum(poses[:, :, images:], axis=0)
    tokens, _ = base.shape
    rows = 64
    for start in range(0, tokens, rows):
        part = pl.ds(start, rows)
        step = (wide(out_p, 1, start, rows) + wide(in_p, 1, start, rows)) * change_p[part, :].astype(F32)
        step += (wide(out_o, 1, start, rows) + wide(in_o, 1, start, rows)) * change_o[part, :].astype(F32)
        step += wide(out_x, 1, start, rows) * change_b[part, :].astype(F32)
        step += wide(in_x, 1, start, rows) * change_n[part, :].astype(F32)
        result[part, :] = base[part, :] + STEP * step


def final_stage(base, sums, changes, poses):
    return pl.pallas_call(
        final_kernel,
        in_specs=[VMEM] * 14,
        out_specs=(VMEM, VMEM),
        out_shape=(
            jax.ShapeDtypeStruct(base.shape, F32),
            jax.ShapeDtypeStruct((2, poses.shape[0]), F32),
        ),
        compiler_params=params(),
        name="final_stage",
    )(base, *sums, *changes, poses)


def swap_inner(value):
    return lax.ppermute(value, "img", [(i, i ^ 1) for i in range(lax.axis_size("img"))])


def swap_outer(value):
    count = lax.axis_size("img")
    pairs = [(i, (i + 1) % count) for i in range(1, count, 2)]
    return lax.ppermute(value, "img", pairs + [(b, a) for a, b in pairs])


def along(value, by):
    count = lax.axis_size("group")
    return lax.ppermute(value, "group", [(i, (i + by) % count) for i in range(count)])


def local(
    enc_tokens,
    embed_weight,
    embed_bias,
    query_gain,
    memory_gain,
    query_weight,
    key_weight,
    value_weight,
    out_weight,
    head_weight,
    pair_dst,
    pair_count,
    depth,
    scale,
    focal,
):
    tokens = enc_tokens.shape[1]
    half = tokens // 2
    depth_now = depth[0]
    embed, rows, short = embed_stage(
        enc_tokens[0], embed_weight, embed_bias, memory_gain, depth_now
    )
    rows_x = along(rows, 1)
    rows_o = swap_outer(rows)
    rows_p = swap_inner(rows)
    late_x = along(short, 1)
    query_t, value_wt, peak = query_stage(embed, query_gain, query_weight, value_weight)
    common = (pair_dst, pair_count, scale, focal, query_t, peak, embed, out_weight, head_weight, depth_now)
    weights = (key_weight, value_wt)
    kept, sent_p, moved_p = pair_stage(1, 0, tokens, common, (rows_p, *weights))
    in_p = swap_inner(sent_p)
    kept, sent_o, moved_o = pair_stage(2, 0, tokens, common, (rows_o, *weights), kept)
    in_o = swap_outer(sent_o)
    kept, sent_a, moved_a, *made_x = pair_stage(3, 0, half, common, (rows_x, *weights), kept, True)
    in_a = along(sent_a, -1)
    kept, sent_b, moved_b = pair_stage(3, half, tokens - half, common, made_x, kept)
    in_b = along(sent_b, -1)
    sums = (sent_a, sent_b, in_a, in_b, sent_o, in_o, sent_p, in_p)
    moved = (moved_a, moved_b, moved_o, moved_p)
    base, change, poses = align_stage(scale, focal, depth_now, *moved, *sums, late_x)
    changes = (swap_inner(change), swap_outer(change), along(change, 1), along(change, -1))
    poses = lax.all_to_all(poses, ("group", "img"), 0, 0, tiled=True)
    depth_out, pose = final_stage(base, sums, changes, poses)
    return (kept, depth_out[None], pose[0], pose[1])


def solution(mesh):
    whole = P(("group", "img"), None, None)
    line = P(("group", "img"))
    return jax.shard_map(
        local,
        mesh=mesh,
        in_specs=(whole, *[P()] * 9, line, line, whole, P(), P()),
        out_specs=(whole, whole, P(), P()),
        check_vma=False,
    )
```

```python
import jax
import jax.numpy as jnp
from jax import lax
from jax.experimental import pallas as pl
from jax.experimental.pallas import tpu as pltpu
from jax.sharding import PartitionSpec as P

HEADS = 12
HEAD = 64
STEP = 0.1
FAST = 3
LOG2E = 1.4426950408889634
F32 = jnp.float32
BF16 = jnp.bfloat16


def matmul(a, b, left=1, right=0):
    return lax.dot_general(a, b, (((left,), (right,)), ((), ())), preferred_element_type=F32)


def ramp_of(start, rows, width, total):
    row = lax.broadcasted_iota(jnp.int32, (rows, width), 0) + start
    col = lax.broadcasted_iota(jnp.int32, (rows, width), 1)
    return 2.0 * ((row * width + col).astype(F32) + 0.5) / total - 1.0


def params(mebi=24):
    return pltpu.CompilerParams(vmem_limit_bytes=mebi << 20)


VMEM = pl.BlockSpec(memory_space=pltpu.VMEM)
SMEM = pl.BlockSpec(memory_space=pltpu.SMEM)
HBM = pl.BlockSpec(memory_space=pl.ANY)


def neighbours():
    group_count, img_count = lax.axis_size("group"), lax.axis_size("img")
    group, img = lax.axis_index("group"), lax.axis_index("img")
    base = group * img_count
    inner = base + img + 1 - 2 * (img % 2)
    outer = base + jnp.clip(img - 1 + 2 * (img % 2), 0, img_count - 1)
    back = (group + group_count - 1) % group_count * img_count + img
    ahead = (group + 1) % group_count * img_count + img
    return base + img, inner, outer, back, ahead


def normed(value, gain):
    value = value.astype(F32)
    center = value - jnp.mean(value, axis=-1, keepdims=True)
    spread = jnp.mean(center * center, axis=-1, keepdims=True)
    return (center * lax.rsqrt(spread + 1e-05) * gain).astype(BF16)


def embed_kernel(enc, weight, bias, memory_gain, depth, embed, rows_out, late, *scratch):
    enc_v, weight_v, depth_v, bias_v, gain_v, embed_v, rows_v, late_v, arrive, leave = scratch
    tokens = embed.shape[0]
    count = 3
    rows = tokens // count
    moves = [pltpu.make_async_copy(weight, weight_v, arrive.at[0])]
    for index in range(count):
        part = pl.ds(index * rows, rows)
        moves.append(pltpu.make_async_copy(enc.at[part], enc_v.at[part], arrive.at[index + 1]))
    for place, pair in enumerate(((bias, bias_v), (memory_gain, gain_v), (depth, depth_v))):
        moves.append(pltpu.make_async_copy(*pair, arrive.at[count + 1 + place]))
    for move in moves:
        move.start()
    for move in (moves[0], moves[count + 1], moves[count + 2]):
        move.wait()
    out = []
    for index in range(count):
        part = pl.ds(index * rows, rows)
        moves[index + 1].wait()
        value = (matmul(enc_v[part, :], weight_v[...]) + bias_v[...][None, :]).astype(BF16)
        embed_v[part, :] = value
        rows_v[part, :] = normed(value, gain_v[...][None, :])
        for place, (source, target) in enumerate(((rows_v, rows_out), (embed_v, embed))):
            out.append(pltpu.make_async_copy(source.at[part], target.at[part], leave.at[index * 2 + place]))
            out[-1].start()
    moves[-1].wait()
    late_v[...] = depth_v[...].astype(BF16)
    out.append(pltpu.make_async_copy(late_v, late, leave.at[count * 2]))
    out[-1].start()
    for move in out:
        move.wait()


def embed_stage(enc, weight, bias, memory_gain, depth):
    tokens, width = enc.shape[0], weight.shape[1]
    patch = depth.shape[1]
    shapes = [(tokens, width), (tokens, width), (tokens, patch)]
    return pl.pallas_call(
        embed_kernel,
        in_specs=[HBM] * 5,
        out_specs=(HBM,) * 3,
        out_shape=tuple(jax.ShapeDtypeStruct(shape, BF16) for shape in shapes),
        scratch_shapes=[
            pltpu.VMEM(enc.shape, BF16),
            pltpu.VMEM(weight.shape, BF16),
            pltpu.VMEM(depth.shape, F32),
            pltpu.VMEM(bias.shape, F32),
            pltpu.VMEM(bias.shape, F32),
            *[pltpu.VMEM(shape, BF16) for shape in shapes],
            pltpu.SemaphoreType.DMA((7,)),
            pltpu.SemaphoreType.DMA((7,)),
        ],
        compiler_params=params(),
        name="embed_stage",
    )(*[pltpu.with_memory_space_constraint(array, pltpu.HBM) for array in (enc, weight, bias, memory_gain, depth)])


def query_kernel(embed, gain, query_w, value_w, query_t, value_wt, peak):
    scaled = HEAD**-0.5 * LOG2E
    value_wt[...] = value_w[...].T
    rows = 256
    largest = jnp.float32(0.0)
    for start in range(0, embed.shape[0], rows):
        part = pl.ds(start, rows)
        value = normed(embed[part, :], gain[...][None, :])
        query = (matmul(query_w[...], value, 0, 1) * scaled).astype(BF16)
        query_t[:, part] = query
        query = query.astype(F32)
        norm = jnp.sum((query * query).reshape(HEADS, HEAD, rows), axis=1)
        largest = jnp.maximum(largest, jnp.max(norm))
    peak[...] = jnp.full(peak.shape, largest, F32)


def query_stage(embed, gain, query_w, value_w):
    return pl.pallas_call(
        query_kernel,
        in_specs=[VMEM] * 4,
        out_specs=(VMEM,) * 3,
        out_shape=(
            jax.ShapeDtypeStruct(embed.shape[::-1], BF16),
            jax.ShapeDtypeStruct(value_w.shape[::-1], BF16),
            jax.ShapeDtypeStruct((8, 128), F32),
        ),
        compiler_params=params(),
        name="query_stage",
    )(embed, gain, query_w, value_w)


def attention(query_t, keys, values_t, mixed_t, first, count, group, shifted):
    def scores(base, half):
        offset = pl.multiple_of(base + half * HEAD, HEAD)
        query = query_t[pl.ds(offset, HEAD), pl.ds(first, count)]
        blank = jnp.zeros_like(query)
        both = jnp.concatenate([query, blank] if half == 0 else [blank, query], axis=0)
        return matmul(keys[:, pl.ds(base, 2 * HEAD)], both), offset

    def finish(score, offset):
        if shifted:
            score = score - jnp.max(score, axis=0, keepdims=True)
        probs = jnp.exp2(score).astype(BF16)
        ones = jnp.ones((16, keys.shape[0]), BF16)
        stacked = jnp.concatenate([values_t[pl.ds(offset, HEAD), :], ones], axis=0)
        mixed = matmul(stacked, probs)
        mixed_t[pl.ds(offset, HEAD), :] = (mixed[:HEAD] * (1.0 / mixed[HEAD : HEAD + 1])).astype(BF16)

    def single(head, carry):
        base = pl.multiple_of(head // 2 * 2 * HEAD, 2 * HEAD)
        both = query_t[pl.ds(base, 2 * HEAD), pl.ds(first, count)]
        row = lax.broadcasted_iota(jnp.int32, both.shape, 0) // HEAD
        both = jnp.where(row == head % 2, both, jnp.zeros_like(both))
        finish(matmul(keys[:, pl.ds(base, 2 * HEAD)], both), pl.multiple_of(head * HEAD, HEAD))
        return carry

    def step(index, carry):
        pending = None
        for pair in range(group):
            base = pl.multiple_of((index * group + pair) * 2 * HEAD, 2 * HEAD)
            for half in range(2):
                current = scores(base, half)
                if pending is not None:
                    finish(*pending)
                pending = current
        finish(*pending)
        return carry

    if shifted:
        lax.fori_loop(0, HEADS, single, 0)
    else:
        lax.fori_loop(0, HEADS // 2 // group, step, 0)


def key_peak(keys):
    width = keys.shape[1]
    square = keys[...].astype(F32)
    square = (square * square).astype(BF16)
    row = lax.broadcasted_iota(jnp.int32, (width, 128), 0) // HEAD
    col = lax.broadcasted_iota(jnp.int32, (width, 128), 1)
    return jnp.max(matmul(square, jnp.where(row == col, 1.0, 0.0).astype(BF16)))


def pair_kernel(which, first, count, make, keep, chained, *refs):
    refs = list(refs)

    def take(number):
        return [refs.pop(0) for _ in range(number)]

    dst, live, scale, focal, query_t, peak, embed, out_w, head_w, depth = take(10)
    if make:
        packed, key_w, value_wt = take(3)
    else:
        keys, values_t, reach = take(3)
    if chained:
        take(1)
    pair_tokens, sent, moved_out = take(3)
    if make:
        keys, values_t = take(2)
        reach = take(1)[0] if keep else None
    mixed_t, rows_out, sems = take(3)
    zeros = None if chained else take(1)[0]
    tokens, _ = embed.shape
    patch = depth.shape[1]
    slots = pair_tokens.shape[0]
    ids = neighbours()
    own, target = ids[0], ids[which]
    hits = [(dst[slot] == target) & (slot < live[0]) for slot in range(slots)]
    dead = [slot >= live[0] for slot in range(slots)]

    def clear(slot):
        return pltpu.make_async_copy(zeros, pair_tokens.at[slot], sems.at[slot])

    rows = 256 if count % 256 == 0 else 128

    def write(slot, start):
        place = pair_tokens.at[slot, pl.ds(first + start, rows)]
        source = rows_out.at[pl.ds(start, rows)]
        return pltpu.make_async_copy(source, place, sems.at[slots * (1 + start // rows) + slot])

    if not chained:
        zeros[...] = jnp.zeros_like(zeros)
        for slot in range(slots):
            pl.when(dead[slot])(lambda slot=slot: clear(slot).start())
    if make:
        memory = packed[...]
        keys[...] = matmul(memory, key_w[...]).astype(BF16)
        values_t[...] = matmul(value_wt[...], memory, 1, 1).astype(BF16)
        largest = key_peak(keys)
        if keep:
            reach[...] = jnp.full(reach.shape, largest, F32)
    else:
        largest = jnp.max(reach[...])
    small = jnp.max(peak[...]) * largest <= 8000.0

    @pl.when(small)
    def _():
        attention(query_t, keys, values_t, mixed_t, first, count, FAST, False)

    @pl.when(jnp.logical_not(small))
    def _():
        attention(query_t, keys, values_t, mixed_t, first, count, 1, True)

    weight = jnp.float32(0.0)
    for slot in range(slots):
        weight = weight + jnp.where(hits[slot], 1.0, 0.0)
    shift = scale[own] - scale[target]
    tilt = focal[own] - focal[target]
    for start in range(0, count, rows):
        part = pl.ds(start, rows)
        whole = pl.ds(first + start, rows)
        attended = matmul(mixed_t[:, part], out_w[...], 0, 0)
        value = (embed[whole, :].astype(F32) + attended).astype(BF16)
        rows_out[part, :] = value
        for slot in range(slots):
            pl.when(hits[slot])(lambda slot=slot: write(slot, start).start())
        head = matmul(value, head_w[...])
        logit = head[:, patch:]
        soft = jnp.maximum(logit, 0.0) + jnp.log1p(jnp.exp(-jnp.abs(logit)))
        confidence = weight * (0.1 + soft)
        ramp = ramp_of(first + start, rows, patch, tokens * patch)
        moved = confidence * (depth[whole, :] + shift + tilt * ramp - head[:, :patch])
        sent[0, part, :] = moved.astype(BF16)
        sent[1, part, :] = confidence.astype(BF16)
        moved_out[part, :] = moved
        if sent.shape[0] == 3:
            sent[2, part, :] = depth[whole, :].astype(BF16)
    for start in range(0, count, rows):
        for slot in range(slots):
            pl.when(hits[slot])(lambda slot=slot: write(slot, start).wait())
    if not chained:
        for slot in range(slots):
            pl.when(dead[slot])(lambda slot=slot: clear(slot).wait())


def pair_stage(which, first, count, common, source, chain=None, keep=False):
    tokens, width = common[6].shape
    patch = common[9].shape[1]
    slots = common[0].shape[0]
    chained = chain is not None
    make = source[0].shape[0] == tokens and source[2].shape == (width, width)
    operands = [*common, *source]
    specs = [SMEM] * 4 + [VMEM] * (len(operands) - 4)
    if chained:
        operands.append(chain)
        specs.append(HBM)
    kept = ((tokens, width), (width, tokens))
    scratch = [] if keep or not make else [pltpu.VMEM(shape, BF16) for shape in kept]
    scratch += [
        pltpu.VMEM((width, count), BF16),
        pltpu.VMEM((count, width), BF16),
        pltpu.SemaphoreType.DMA((4 * slots,)),
    ]
    if not chained:
        scratch.append(pltpu.VMEM((tokens, width), BF16))
    results = [
        jax.ShapeDtypeStruct((slots, tokens, width), BF16),
        jax.ShapeDtypeStruct((2 if which == 3 else 3, count, patch), BF16),
        jax.ShapeDtypeStruct((count, patch), F32),
    ]
    if keep:
        results += [jax.ShapeDtypeStruct(shape, BF16) for shape in kept]
        results.append(jax.ShapeDtypeStruct((8, 128), F32))

    def body(*refs):
        pair_kernel(which, first, count, make, keep, chained, *refs)

    return pl.pallas_call(
        body,
        in_specs=specs,
        out_specs=(HBM,) + (VMEM,) * (len(results) - 1),
        out_shape=tuple(results),
        scratch_shapes=scratch,
        input_output_aliases={len(operands) - 1: 0} if chained else {},
        compiler_params=params(),
    )(*operands)


def strip(pieces, start, rows, *index):
    for piece in pieces:
        height = piece.shape[-2]
        if start < height:
            return piece[(*index, pl.ds(start, rows), slice(None))].astype(F32)
        start -= height


def wide(pieces, index, start, rows):
    return strip(pieces, start, rows, index)


def gather_kernel(depth, *refs):
    moved_x, (moved_o, moved_p), out_x = [refs[2 * index : 2 * index + 2] for index in range(3)]
    moved_o, moved_p = (moved_o,), (moved_p,)
    out_o, in_o, out_p, in_p, late = [refs[index : index + 1] for index in range(6, 11)]
    total, link_o, link_p = refs[11:]
    rows = 64
    for start in range(0, depth.shape[0], rows):
        part = pl.ds(start, rows)
        own = depth[part, :]
        grad = strip(moved_x, start, rows) + strip(moved_o, start, rows) + strip(moved_p, start, rows)
        grad = grad - wide(out_x, 1, start, rows) * strip(late, start, rows)
        for outs, ins, link in ((out_o, in_o, link_o), (out_p, in_p, link_p)):
            back = wide(ins, 1, start, rows)
            ahead = wide(outs, 1, start, rows)
            grad = grad - wide(ins, 0, start, rows) + back * own - ahead * wide(ins, 2, start, rows)
            link[part, :] = back + ahead
        total[part, :] = grad


def gather_stage(depth, *arrays):
    return pl.pallas_call(
        gather_kernel,
        in_specs=[VMEM] * (len(arrays) + 1),
        out_specs=(VMEM,) * 3,
        out_shape=(jax.ShapeDtypeStruct(depth.shape, F32),) * 3,
        compiler_params=params(),
        name="gather_stage",
    )(depth, *arrays)


def align_kernel(scale, focal, depth, total, link_o, link_p, *refs):
    out_x, in_x = refs[0:2], refs[2:4]
    base, change, poses, grads = refs[4:]
    tokens, patch = depth.shape
    pixels = tokens * patch
    rows = 64

    def fold(value):
        return jnp.sum(value.reshape(rows // 8, 8, patch), axis=0)

    plain = jnp.zeros((8, patch), F32)
    slope = jnp.zeros((8, patch), F32)
    for start in range(0, tokens, rows):
        part = pl.ds(start, rows)
        grad = total[part, :] - wide(in_x, 0, start, rows) + wide(in_x, 1, start, rows) * depth[part, :]
        grads[pl.ds(start, rows), :] = grad
        plain = plain + fold(grad)
        slope = slope + fold(grad * ramp_of(start, rows, patch, pixels))
    plain = jnp.sum(plain) / pixels
    slope = jnp.sum(slope) / pixels
    sums = [jnp.zeros((8, patch), F32) for _ in range(8)]
    for start in range(0, tokens, rows):
        part = pl.ds(start, rows)
        grad = grads[part, :]
        ramp = ramp_of(start, rows, patch, pixels)
        delta = -STEP * (grad + plain + slope * ramp)
        change[part, :] = delta.astype(BF16)
        links = [
            link_p[part, :],
            link_o[part, :],
            wide(out_x, 1, start, rows),
            wide(in_x, 1, start, rows),
        ]
        shares = [link * delta for link in links]
        base[part, :] = depth[part, :] - STEP * (
            2.0 * grad + (shares[0] + shares[1] + shares[2] + shares[3])
        )
        for index in range(4):
            sums[index] = sums[index] + fold(shares[index])
            sums[index + 4] = sums[index + 4] + fold(shares[index] * ramp)
    sums = [jnp.sum(value) / pixels for value in sums]
    ids = neighbours()
    lane = lax.broadcasted_iota(jnp.int32, (1, poses.shape[0]), 1)

    def spread(start, first, parts):
        own = start - STEP * (2.0 * first + (parts[0] + parts[1] + parts[2] + parts[3]))
        row = jnp.where(lane == ids[0], own, 0.0)
        for index in range(4):
            row = row + jnp.where(lane == ids[index + 1], STEP * parts[index], 0.0)
        return row

    images = lane.shape[1]
    for half, row in enumerate((spread(scale[ids[0]], plain, sums[:4]), spread(focal[ids[0]], slope, sums[4:]))):
        place = slice(half * images, (half + 1) * images)
        poses[:, :, place] = jnp.broadcast_to(row[None], (images, 1, images))


def align_stage(scale, focal, depth, *arrays):
    tokens, patch = depth.shape
    return pl.pallas_call(
        align_kernel,
        in_specs=[SMEM, SMEM] + [VMEM] * (len(arrays) + 1),
        out_specs=(VMEM, VMEM, VMEM),
        out_shape=(
            jax.ShapeDtypeStruct((tokens, patch), F32),
            jax.ShapeDtypeStruct((tokens, patch), BF16),
            jax.ShapeDtypeStruct((scale.shape[0], 1, 2 * scale.shape[0]), F32),
        ),
        scratch_shapes=[pltpu.VMEM((tokens, patch), F32)],
        compiler_params=params(),
        name="align_stage",
    )(scale, focal, depth, *arrays)


def final_kernel(base, *refs):
    link_o, link_p = refs[:2]
    out_x, in_x = refs[2:4], refs[4:6]
    change_p, change_o, change_b, change_n, poses, result, pose_a, pose_f = refs[6:]
    images = poses.shape[0]
    pose_a[...] = jnp.sum(poses[:, :, :images], axis=0)[0]
    pose_f[...] = jnp.sum(poses[:, :, images:], axis=0)[0]
    tokens, _ = base.shape
    rows = 64
    for start in range(0, tokens, rows):
        part = pl.ds(start, rows)
        step = link_p[part, :] * change_p[part, :].astype(F32)
        step += link_o[part, :] * change_o[part, :].astype(F32)
        step += wide(out_x, 1, start, rows) * change_b[part, :].astype(F32)
        step += wide(in_x, 1, start, rows) * change_n[part, :].astype(F32)
        result[part, :] = base[part, :] + STEP * step


def final_stage(base, sums, changes, poses):
    return pl.pallas_call(
        final_kernel,
        in_specs=[VMEM] * 12,
        out_specs=(VMEM,) * 3,
        out_shape=(
            jax.ShapeDtypeStruct(base.shape, F32),
            jax.ShapeDtypeStruct((poses.shape[0],), F32),
            jax.ShapeDtypeStruct((poses.shape[0],), F32),
        ),
        compiler_params=params(),
        name="final_stage",
    )(base, *sums, *changes, poses)


def swap_inner(value):
    return lax.ppermute(value, "img", [(i, i ^ 1) for i in range(lax.axis_size("img"))])


def swap_outer(value):
    count = lax.axis_size("img")
    pairs = [(i, (i + 1) % count) for i in range(1, count, 2)]
    return lax.ppermute(value, "img", pairs + [(b, a) for a, b in pairs])


def along(value, by):
    count = lax.axis_size("group")
    return lax.ppermute(value, "group", [(i, (i + by) % count) for i in range(count)])


def local(
    enc_tokens,
    embed_weight,
    embed_bias,
    query_gain,
    memory_gain,
    query_weight,
    key_weight,
    value_weight,
    out_weight,
    head_weight,
    pair_dst,
    pair_count,
    depth,
    scale,
    focal,
):
    tokens = enc_tokens.shape[1]
    half = tokens // 2
    depth_now = depth[0]
    embed, rows, short = embed_stage(
        enc_tokens[0], embed_weight, embed_bias, memory_gain, depth_now
    )
    rows_x = along(rows, 1)
    rows_o = swap_outer(rows)
    rows_p = swap_inner(rows)
    late_x = along(short, 1)
    query_t, value_wt, peak = query_stage(embed, query_gain, query_weight, value_weight)
    common = (pair_dst, pair_count, scale, focal, query_t, peak, embed, out_weight, head_weight, depth_now)
    weights = (key_weight, value_wt)
    kept, sent_p, moved_p = pair_stage(1, 0, tokens, common, (rows_p, *weights))
    in_p = swap_inner(sent_p)
    kept, sent_o, moved_o = pair_stage(2, 0, tokens, common, (rows_o, *weights), kept)
    in_o = swap_outer(sent_o)
    kept, sent_a, moved_a, *made_x = pair_stage(3, 0, half, common, (rows_x, *weights), kept, True)
    in_a = along(sent_a, -1)
    kept, sent_b, moved_b = pair_stage(3, half, tokens - half, common, made_x, kept)
    in_b = along(sent_b, -1)
    moved = (moved_a, moved_b, moved_o, moved_p)
    total, *links = gather_stage(depth_now, *moved, sent_a, sent_b, sent_o, in_o, sent_p, in_p, late_x)
    sums = (*links, sent_a, sent_b, in_a, in_b)
    base, change, poses = align_stage(scale, focal, depth_now, total, *sums)
    changes = (swap_inner(change), swap_outer(change), along(change, 1), along(change, -1))
    poses = lax.all_to_all(poses, ("group", "img"), 0, 0, tiled=True)
    depth_out, pose_a, pose_f = final_stage(base, sums, changes, poses)
    return (kept, depth_out[None], pose_a, pose_f)


def solution(mesh):
    whole = P(("group", "img"), None, None)
    line = P(("group", "img"))
    return jax.shard_map(
        local,
        mesh=mesh,
        in_specs=(whole, *[P()] * 9, line, line, whole, P(), P()),
        out_specs=(whole, whole, P(), P()),
        check_vma=False,
    )
```

```python
import jax
import jax.numpy as jnp
from jax import lax
from jax.experimental import pallas as pl
from jax.experimental.pallas import tpu as pltpu
from jax.sharding import PartitionSpec as P

HEADS = 12
HEAD = 64
STEP = 0.1
FAST = 3
LOG2E = 1.4426950408889634
F32 = jnp.float32
BF16 = jnp.bfloat16


def matmul(a, b, left=1, right=0):
    return lax.dot_general(a, b, (((left,), (right,)), ((), ())), preferred_element_type=F32)


def ramp_of(start, rows, width, total):
    row = lax.broadcasted_iota(jnp.int32, (rows, width), 0) + start
    col = lax.broadcasted_iota(jnp.int32, (rows, width), 1)
    return 2.0 * ((row * width + col).astype(F32) + 0.5) / total - 1.0


def params(mebi=24):
    return pltpu.CompilerParams(vmem_limit_bytes=mebi << 20)


VMEM = pl.BlockSpec(memory_space=pltpu.VMEM)
SMEM = pl.BlockSpec(memory_space=pltpu.SMEM)
HBM = pl.BlockSpec(memory_space=pl.ANY)


def neighbours():
    group_count, img_count = lax.axis_size("group"), lax.axis_size("img")
    group, img = lax.axis_index("group"), lax.axis_index("img")
    base = group * img_count
    inner = base + img + 1 - 2 * (img % 2)
    outer = base + jnp.clip(img - 1 + 2 * (img % 2), 0, img_count - 1)
    back = (group + group_count - 1) % group_count * img_count + img
    ahead = (group + 1) % group_count * img_count + img
    return base + img, inner, outer, back, ahead


def normed(value, gain):
    value = value.astype(F32)
    center = value - jnp.mean(value, axis=-1, keepdims=True)
    spread = jnp.mean(center * center, axis=-1, keepdims=True)
    return (center * lax.rsqrt(spread + 1e-05) * gain).astype(BF16)


def embed_kernel(enc, weight, bias, memory_gain, depth, embed, rows_out, late, *scratch):
    enc_v, weight_v, depth_v, bias_v, gain_v, arrive = scratch
    tokens = embed.shape[0]
    count = 3
    rows = tokens // count
    moves = [pltpu.make_async_copy(weight, weight_v, arrive.at[0])]
    for index in range(count):
        part = pl.ds(index * rows, rows)
        moves.append(pltpu.make_async_copy(enc.at[part], enc_v.at[part], arrive.at[index + 1]))
    for place, pair in enumerate(((bias, bias_v), (memory_gain, gain_v), (depth, depth_v))):
        moves.append(pltpu.make_async_copy(*pair, arrive.at[count + 1 + place]))
    early = (moves[0], moves[1], moves[count + 1], moves[count + 2])
    for move in early:
        move.start()
    moves[0].wait()
    for move in (*moves[2 : count + 1], moves[-1]):
        move.start()
    for move in early[2:]:
        move.wait()
    for index in range(count):
        part = pl.ds(index * rows, rows)
        moves[index + 1].wait()
        value = (matmul(enc_v[part, :], weight_v[...]) + bias_v[...][None, :]).astype(BF16)
        embed[part, :] = value
        rows_out[part, :] = normed(value, gain_v[...][None, :])
    moves[-1].wait()
    late[...] = depth_v[...].astype(BF16)


def embed_stage(enc, weight, bias, memory_gain, depth):
    tokens, width = enc.shape[0], weight.shape[1]
    patch = depth.shape[1]
    shapes = [(tokens, width), (tokens, width), (tokens, patch)]
    return pl.pallas_call(
        embed_kernel,
        in_specs=[HBM] * 5,
        out_specs=(VMEM,) * 3,
        out_shape=tuple(jax.ShapeDtypeStruct(shape, BF16) for shape in shapes),
        scratch_shapes=[
            pltpu.VMEM(enc.shape, BF16),
            pltpu.VMEM(weight.shape, BF16),
            pltpu.VMEM(depth.shape, F32),
            pltpu.VMEM(bias.shape, F32),
            pltpu.VMEM(bias.shape, F32),
            pltpu.SemaphoreType.DMA((7,)),
        ],
        compiler_params=params(),
        name="embed_stage",
    )(*[pltpu.with_memory_space_constraint(array, pltpu.HBM) for array in (enc, weight, bias, memory_gain, depth)])


def query_kernel(embed, gain, query_w, value_w, query_t, value_wt, peak):
    scaled = HEAD**-0.5 * LOG2E
    value_wt[...] = value_w[...].T
    rows = 256
    largest = jnp.float32(0.0)
    for start in range(0, embed.shape[0], rows):
        part = pl.ds(start, rows)
        value = normed(embed[part, :], gain[...][None, :])
        query = (matmul(query_w[...], value, 0, 1) * scaled).astype(BF16)
        query_t[:, part] = query
        query = query.astype(F32)
        norm = jnp.sum((query * query).reshape(HEADS, HEAD, rows), axis=1)
        largest = jnp.maximum(largest, jnp.max(norm))
    peak[...] = jnp.full(peak.shape, largest, F32)


def query_stage(embed, gain, query_w, value_w):
    return pl.pallas_call(
        query_kernel,
        in_specs=[VMEM] * 4,
        out_specs=(VMEM,) * 3,
        out_shape=(
            jax.ShapeDtypeStruct(embed.shape[::-1], BF16),
            jax.ShapeDtypeStruct(value_w.shape[::-1], BF16),
            jax.ShapeDtypeStruct((8, 128), F32),
        ),
        compiler_params=params(),
        name="query_stage",
    )(embed, gain, query_w, value_w)


def attention(query_t, keys, values_t, mixed_t, first, count, group, shifted):
    def scores(base, half):
        offset = pl.multiple_of(base + half * HEAD, HEAD)
        query = query_t[pl.ds(offset, HEAD), pl.ds(first, count)]
        blank = jnp.zeros_like(query)
        both = jnp.concatenate([query, blank] if half == 0 else [blank, query], axis=0)
        return matmul(keys[:, pl.ds(base, 2 * HEAD)], both), offset

    def finish(score, offset):
        if shifted:
            score = score - jnp.max(score, axis=0, keepdims=True)
        probs = jnp.exp2(score).astype(BF16)
        ones = jnp.ones((16, keys.shape[0]), BF16)
        stacked = jnp.concatenate([values_t[pl.ds(offset, HEAD), :], ones], axis=0)
        mixed = matmul(stacked, probs)
        mixed_t[pl.ds(offset, HEAD), :] = (mixed[:HEAD] * (1.0 / mixed[HEAD : HEAD + 1])).astype(BF16)

    def single(head, carry):
        base = pl.multiple_of(head // 2 * 2 * HEAD, 2 * HEAD)
        both = query_t[pl.ds(base, 2 * HEAD), pl.ds(first, count)]
        row = lax.broadcasted_iota(jnp.int32, both.shape, 0) // HEAD
        both = jnp.where(row == head % 2, both, jnp.zeros_like(both))
        finish(matmul(keys[:, pl.ds(base, 2 * HEAD)], both), pl.multiple_of(head * HEAD, HEAD))
        return carry

    def step(index, carry):
        pending = None
        for pair in range(group):
            base = pl.multiple_of((index * group + pair) * 2 * HEAD, 2 * HEAD)
            for half in range(2):
                current = scores(base, half)
                if pending is not None:
                    finish(*pending)
                pending = current
        finish(*pending)
        return carry

    if shifted:
        lax.fori_loop(0, HEADS, single, 0)
    else:
        lax.fori_loop(0, HEADS // 2 // group, step, 0)


def key_peak(keys):
    width = keys.shape[1]
    square = keys[...].astype(F32)
    square = (square * square).astype(BF16)
    row = lax.broadcasted_iota(jnp.int32, (width, 128), 0) // HEAD
    col = lax.broadcasted_iota(jnp.int32, (width, 128), 1)
    return jnp.max(matmul(square, jnp.where(row == col, 1.0, 0.0).astype(BF16)))


def pair_kernel(which, first, count, make, keep, chained, *refs):
    refs = list(refs)

    def take(number):
        return [refs.pop(0) for _ in range(number)]

    dst, live, scale, focal, query_t, peak, embed, out_w, head_w, depth = take(10)
    if make:
        packed, key_w, value_wt = take(3)
    else:
        keys, values_t, reach = take(3)
    if chained:
        take(1)
    pair_tokens, sent, moved_out = take(3)
    if make:
        keys, values_t = take(2)
        reach = take(1)[0] if keep else None
    mixed_t, rows_out, sems = take(3)
    zeros = None if chained else take(1)[0]
    tokens, _ = embed.shape
    patch = depth.shape[1]
    slots = pair_tokens.shape[0]
    ids = neighbours()
    own, target = ids[0], ids[which]
    hits = [(dst[slot] == target) & (slot < live[0]) for slot in range(slots)]
    dead = [slot >= live[0] for slot in range(slots)]

    def clear(slot):
        return pltpu.make_async_copy(zeros, pair_tokens.at[slot], sems.at[slot])

    rows = 384

    def write(slot, start):
        place = pair_tokens.at[slot, pl.ds(first + start, rows)]
        source = rows_out.at[pl.ds(start, rows)]
        return pltpu.make_async_copy(source, place, sems.at[slots * (1 + start // rows) + slot])

    if not chained:
        zeros[...] = jnp.zeros_like(zeros)
        for slot in range(slots):
            pl.when(dead[slot])(lambda slot=slot: clear(slot).start())
    if make:
        memory = packed[...]
        keys[...] = matmul(memory, key_w[...]).astype(BF16)
        values_t[...] = matmul(value_wt[...], memory, 1, 1).astype(BF16)
        largest = key_peak(keys)
        if keep:
            reach[...] = jnp.full(reach.shape, largest, F32)
    else:
        largest = jnp.max(reach[...])
    small = jnp.max(peak[...]) * largest <= 8000.0

    @pl.when(small)
    def _():
        attention(query_t, keys, values_t, mixed_t, first, count, FAST, False)

    @pl.when(jnp.logical_not(small))
    def _():
        attention(query_t, keys, values_t, mixed_t, first, count, 1, True)

    weight = jnp.float32(0.0)
    for slot in range(slots):
        weight = weight + jnp.where(hits[slot], 1.0, 0.0)
    shift = scale[own] - scale[target]
    tilt = focal[own] - focal[target]
    for start in range(0, count, rows):
        part = pl.ds(start, rows)
        whole = pl.ds(first + start, rows)
        attended = matmul(mixed_t[:, part], out_w[...], 0, 0)
        value = (embed[whole, :].astype(F32) + attended).astype(BF16)
        rows_out[part, :] = value
        for slot in range(slots):
            pl.when(hits[slot])(lambda slot=slot: write(slot, start).start())
        head = matmul(value, head_w[...])
        logit = head[:, patch:]
        soft = jnp.maximum(logit, 0.0) + jnp.log1p(jnp.exp(-jnp.abs(logit)))
        confidence = weight * (0.1 + soft)
        ramp = ramp_of(first + start, rows, patch, tokens * patch)
        moved = confidence * (depth[whole, :] + shift + tilt * ramp - head[:, :patch])
        sent[0, part, :] = moved.astype(BF16)
        sent[1, part, :] = confidence.astype(BF16)
        moved_out[part, :] = moved
        if sent.shape[0] == 3:
            sent[2, part, :] = depth[whole, :].astype(BF16)
    for start in range(0, count, rows):
        for slot in range(slots):
            pl.when(hits[slot])(lambda slot=slot: write(slot, start).wait())
    if not chained:
        for slot in range(slots):
            pl.when(dead[slot])(lambda slot=slot: clear(slot).wait())


def pair_stage(which, first, count, common, source, chain=None, keep=False):
    tokens, width = common[6].shape
    patch = common[9].shape[1]
    slots = common[0].shape[0]
    chained = chain is not None
    make = source[0].shape[0] == tokens and source[2].shape == (width, width)
    operands = [*common, *source]
    specs = [SMEM] * 4 + [VMEM] * (len(operands) - 4)
    if chained:
        operands.append(chain)
        specs.append(HBM)
    kept = ((tokens, width), (width, tokens))
    scratch = [] if keep or not make else [pltpu.VMEM(shape, BF16) for shape in kept]
    scratch += [
        pltpu.VMEM((width, count), BF16),
        pltpu.VMEM((count, width), BF16),
        pltpu.SemaphoreType.DMA((4 * slots,)),
    ]
    if not chained:
        scratch.append(pltpu.VMEM((tokens, width), BF16))
    results = [
        jax.ShapeDtypeStruct((slots, tokens, width), BF16),
        jax.ShapeDtypeStruct((2 if which == 3 else 3, count, patch), BF16),
        jax.ShapeDtypeStruct((count, patch), F32),
    ]
    if keep:
        results += [jax.ShapeDtypeStruct(shape, BF16) for shape in kept]
        results.append(jax.ShapeDtypeStruct((8, 128), F32))

    def body(*refs):
        pair_kernel(which, first, count, make, keep, chained, *refs)

    return pl.pallas_call(
        body,
        in_specs=specs,
        out_specs=(HBM,) + (VMEM,) * (len(results) - 1),
        out_shape=tuple(results),
        scratch_shapes=scratch,
        input_output_aliases={len(operands) - 1: 0} if chained else {},
        compiler_params=params(),
    )(*operands)


def strip(pieces, start, rows, *index):
    for piece in pieces:
        height = piece.shape[-2]
        if start < height:
            return piece[(*index, pl.ds(start, rows), slice(None))].astype(F32)
        start -= height


def wide(pieces, index, start, rows):
    return strip(pieces, start, rows, index)


def gather_kernel(depth, *refs):
    moved_x, (moved_o, moved_p), out_x = [refs[2 * index : 2 * index + 2] for index in range(3)]
    moved_o, moved_p = (moved_o,), (moved_p,)
    out_o, in_o, out_p, in_p, late = [refs[index : index + 1] for index in range(6, 11)]
    total, link_o, link_p = refs[11:]
    rows = 64
    for start in range(0, depth.shape[0], rows):
        part = pl.ds(start, rows)
        own = depth[part, :]
        grad = strip(moved_x, start, rows) + strip(moved_o, start, rows) + strip(moved_p, start, rows)
        grad = grad - wide(out_x, 1, start, rows) * strip(late, start, rows)
        for outs, ins, link in ((out_o, in_o, link_o), (out_p, in_p, link_p)):
            back = wide(ins, 1, start, rows)
            ahead = wide(outs, 1, start, rows)
            grad = grad - wide(ins, 0, start, rows) + back * own - ahead * wide(ins, 2, start, rows)
            link[part, :] = back + ahead
        total[part, :] = grad


def gather_stage(depth, *arrays):
    return pl.pallas_call(
        gather_kernel,
        in_specs=[VMEM] * (len(arrays) + 1),
        out_specs=(VMEM,) * 3,
        out_shape=(jax.ShapeDtypeStruct(depth.shape, F32),) * 3,
        compiler_params=params(),
        name="gather_stage",
    )(depth, *arrays)


def align_kernel(scale, focal, depth, total, link_o, link_p, *refs):
    out_x, in_x = refs[0:2], refs[2:4]
    base, change, poses, grads = refs[4:]
    tokens, patch = depth.shape
    pixels = tokens * patch
    rows = 64

    def fold(value):
        return jnp.sum(value.reshape(rows // 8, 8, patch), axis=0)

    plain = jnp.zeros((8, patch), F32)
    slope = jnp.zeros((8, patch), F32)
    for start in range(0, tokens, rows):
        part = pl.ds(start, rows)
        grad = total[part, :] - wide(in_x, 0, start, rows) + wide(in_x, 1, start, rows) * depth[part, :]
        grads[pl.ds(start, rows), :] = grad
        plain = plain + fold(grad)
        slope = slope + fold(grad * ramp_of(start, rows, patch, pixels))
    plain = jnp.sum(plain) / pixels
    slope = jnp.sum(slope) / pixels
    sums = [jnp.zeros((8, patch), F32) for _ in range(8)]
    for start in range(0, tokens, rows):
        part = pl.ds(start, rows)
        grad = grads[part, :]
        ramp = ramp_of(start, rows, patch, pixels)
        delta = -STEP * (grad + plain + slope * ramp)
        change[part, :] = delta.astype(BF16)
        links = [
            link_p[part, :],
            link_o[part, :],
            wide(out_x, 1, start, rows),
            wide(in_x, 1, start, rows),
        ]
        shares = [link * delta for link in links]
        base[part, :] = depth[part, :] - STEP * (
            2.0 * grad + (shares[0] + shares[1] + shares[2] + shares[3])
        )
        for index in range(4):
            sums[index] = sums[index] + fold(shares[index])
            sums[index + 4] = sums[index + 4] + fold(shares[index] * ramp)
    sums = [jnp.sum(value) / pixels for value in sums]
    ids = neighbours()
    lane = lax.broadcasted_iota(jnp.int32, (1, poses.shape[0]), 1)

    def spread(start, first, parts):
        own = start - STEP * (2.0 * first + (parts[0] + parts[1] + parts[2] + parts[3]))
        row = jnp.where(lane == ids[0], own, 0.0)
        for index in range(4):
            row = row + jnp.where(lane == ids[index + 1], STEP * parts[index], 0.0)
        return row

    images = lane.shape[1]
    for half, row in enumerate((spread(scale[ids[0]], plain, sums[:4]), spread(focal[ids[0]], slope, sums[4:]))):
        place = slice(half * images, (half + 1) * images)
        poses[:, :, place] = jnp.broadcast_to(row[None], (images, 1, images))


def align_stage(scale, focal, depth, *arrays):
    tokens, patch = depth.shape
    return pl.pallas_call(
        align_kernel,
        in_specs=[SMEM, SMEM] + [VMEM] * (len(arrays) + 1),
        out_specs=(VMEM, VMEM, VMEM),
        out_shape=(
            jax.ShapeDtypeStruct((tokens, patch), F32),
            jax.ShapeDtypeStruct((tokens, patch), BF16),
            jax.ShapeDtypeStruct((scale.shape[0], 1, 2 * scale.shape[0]), F32),
        ),
        scratch_shapes=[pltpu.VMEM((tokens, patch), F32)],
        compiler_params=params(),
        name="align_stage",
    )(scale, focal, depth, *arrays)


def final_kernel(base, *refs):
    link_o, link_p = refs[:2]
    out_x, in_x = refs[2:4], refs[4:6]
    change_p, change_o, change_b, change_n, poses, result, pose_a, pose_f = refs[6:]
    images = poses.shape[0]
    pose_a[...] = jnp.sum(poses[:, :, :images], axis=0)[0]
    pose_f[...] = jnp.sum(poses[:, :, images:], axis=0)[0]
    tokens, _ = base.shape
    rows = 64
    for start in range(0, tokens, rows):
        part = pl.ds(start, rows)
        step = link_p[part, :] * change_p[part, :].astype(F32)
        step += link_o[part, :] * change_o[part, :].astype(F32)
        step += wide(out_x, 1, start, rows) * change_b[part, :].astype(F32)
        step += wide(in_x, 1, start, rows) * change_n[part, :].astype(F32)
        result[part, :] = base[part, :] + STEP * step


def final_stage(base, sums, changes, poses):
    return pl.pallas_call(
        final_kernel,
        in_specs=[VMEM] * 12,
        out_specs=(VMEM,) * 3,
        out_shape=(
            jax.ShapeDtypeStruct(base.shape, F32),
            jax.ShapeDtypeStruct((poses.shape[0],), F32),
            jax.ShapeDtypeStruct((poses.shape[0],), F32),
        ),
        compiler_params=params(),
        name="final_stage",
    )(base, *sums, *changes, poses)


def swap_inner(value):
    return lax.ppermute(value, "img", [(i, i ^ 1) for i in range(lax.axis_size("img"))])


def swap_outer(value):
    count = lax.axis_size("img")
    pairs = [(i, (i + 1) % count) for i in range(1, count, 2)]
    return lax.ppermute(value, "img", pairs + [(b, a) for a, b in pairs])


def along(value, by):
    count = lax.axis_size("group")
    return lax.ppermute(value, "group", [(i, (i + by) % count) for i in range(count)])


def local(
    enc_tokens,
    embed_weight,
    embed_bias,
    query_gain,
    memory_gain,
    query_weight,
    key_weight,
    value_weight,
    out_weight,
    head_weight,
    pair_dst,
    pair_count,
    depth,
    scale,
    focal,
):
    tokens = enc_tokens.shape[1]
    half = tokens // 2
    depth_now = depth[0]
    embed, rows, short = embed_stage(
        enc_tokens[0], embed_weight, embed_bias, memory_gain, depth_now
    )
    rows_x = along(rows, 1)
    rows_o = swap_outer(rows)
    rows_p = swap_inner(rows)
    late_x = along(short, 1)
    query_t, value_wt, peak = query_stage(embed, query_gain, query_weight, value_weight)
    common = (pair_dst, pair_count, scale, focal, query_t, peak, embed, out_weight, head_weight, depth_now)
    weights = (key_weight, value_wt)
    kept, sent_p, moved_p = pair_stage(1, 0, tokens, common, (rows_p, *weights))
    in_p = swap_inner(sent_p)
    kept, sent_o, moved_o = pair_stage(2, 0, tokens, common, (rows_o, *weights), kept)
    in_o = swap_outer(sent_o)
    kept, sent_a, moved_a, *made_x = pair_stage(3, 0, half, common, (rows_x, *weights), kept, True)
    in_a = along(sent_a, -1)
    kept, sent_b, moved_b = pair_stage(3, half, tokens - half, common, made_x, kept)
    in_b = along(sent_b, -1)
    moved = (moved_a, moved_b, moved_o, moved_p)
    total, *links = gather_stage(depth_now, *moved, sent_a, sent_b, sent_o, in_o, sent_p, in_p, late_x)
    sums = (*links, sent_a, sent_b, in_a, in_b)
    base, change, poses = align_stage(scale, focal, depth_now, total, *sums)
    changes = (swap_inner(change), swap_outer(change), along(change, 1), along(change, -1))
    poses = lax.all_to_all(poses, ("group", "img"), 0, 0, tiled=True)
    depth_out, pose_a, pose_f = final_stage(base, sums, changes, poses)
    return (kept, depth_out[None], pose_a, pose_f)


def solution(mesh):
    whole = P(("group", "img"), None, None)
    line = P(("group", "img"))
    return jax.shard_map(
        local,
        mesh=mesh,
        in_specs=(whole, *[P()] * 9, line, line, whole, P(), P()),
        out_specs=(whole, whole, P(), P()),
        check_vma=False,
    )
```
